32 devices in a mesh: lat: 8 (over z, core), lon: 4 (over y, x).
Axes of the slice: x: 2, y: 2, z: 4, core: 2. Of those that a mesh axis runs over, the one named last changes fastest.
Arguments:
- atm_flux: bfloat16 [8, 16, 8, 512], P('lat', None, None, 'lon'), may hold values from -6 to 6
- send_tile: int32 [8, 4, 10], P('lat', 'lon'), may hold values from 0 to 15
- recv_tile: int32 [8, 4, 10], P('lat', 'lon'), may hold values from 0 to 64
- remap_weight: bfloat16 [80, 128, 512], P('lat', None, 'lon'), may hold values from -0.5 to 0.5
- tracer: float32 [16, 256, 1024], P(None, 'lat', 'lon'), may hold values from -6 to 6
- diffusivity: float32 [256, 1024], P('lat', 'lon'), may hold values from 0.02 to 0.12
- zonal_velocity: float32 [256, 1024], P('lat', 'lon'), may hold values from -0.25 to 0.25
- merid_velocity: float32 [256, 1024], P('lat', 'lon'), may hold values from -0.25 to 0.25
- ocean_mask: int32 [256, 1024], P('lat', 'lon'), may hold values 0 or 1
- level_proj: float32 [16, 8], replicated, may hold values from -2 to 2
Outputs:
- ocean_flux: float32 [8, 256, 1024], P(None, 'lat', 'lon')
- tracer_out: float32 [16, 256, 1024], P(None, 'lat', 'lon')
The draws below stay inside these ranges and needn't reach their ends.
Inputs may be any that keep to these rules, and one draw needn't show every extreme that they name: `recv_tile`: A slot whose entry is 64 adds to no tile; several slots may add to one ocean tile.
All inputs are finite; a program needn't handle non-finite values. No bound on the sum of `ocean_mask` on one device may be relied on, other than what follows from the above.
Results may differ from the reference program's by a relative error of at most 0.0004.
Values may be sent and summed in bfloat16 or wider, within the bound.
No kernel may reach another device: no remote copies, remote signals or barrier semaphores. Data moves between devices by JAX's collectives and lax.ppermute only.
A program may use at most 64 MiB of HBM per device.

```python
import math
import jax
import jax.numpy as jnp
from jax import lax

NF = 8
TW = 128
OY = 32
OX = 256
LEV = 16
ATD = 16
CAP = 2
REACH = 2
STEPS = 4
SLOTS = 10
OT = 64
NY = 256
NX = 1024
N_LAT = 8
N_LON = 4


def plant(entries, own_key, smallest, high):
    extent = entries.shape
    spot = [jax.random.randint(jax.random.fold_in(own_key, axis), (), 0, extent[axis]) for axis in range(len(extent))]
    entries = entries.at[tuple(spot)].set(smallest)
    longest = extent.index(max(extent))
    spot[longest] = (spot[longest] + 1) % extent[longest]
    return entries.at[tuple(spot)].set(high)


def level_of(key, shape, cuts, smallest, top_value):
    level = 1.0
    for axis_at, parts in cuts:
        steps = jax.random.uniform(jax.random.fold_in(jax.random.fold_in(key, 6), axis_at), (parts,), jnp.float32, smallest / len(cuts), top_value / len(cuts))
        level = level * jnp.repeat(jnp.exp(steps), shape[axis_at] // parts).reshape((-1,) + (1,) * (len(shape) - 1 - axis_at))
    return level


def noise(stream_key, dims, deviation, limit, cuts=(), held_as=jnp.bfloat16):
    entries = deviation * jax.random.normal(stream_key, dims, jnp.float32)
    if cuts:
        entries = entries * level_of(stream_key, dims, cuts, -0.22, 0.18)
    return jnp.clip(entries, -limit, limit).astype(held_as)


def setup_inputs(seed: int = 0) -> dict:
    arg_keys = jax.random.split(jax.random.key(seed), 11)
    atm_flux = noise(arg_keys[0], (N_LAT, ATD, NF, TW * N_LON), 1.0, 6.0, ((0, 8), (3, 4)))
    send_tile = plant(jax.random.randint(arg_keys[1], (N_LAT, N_LON, SLOTS), 0, ATD), jax.random.fold_in(arg_keys[1], 1), 0, ATD - 1).astype(jnp.int32)
    recv_tile = plant(jax.random.randint(arg_keys[2], (N_LAT, N_LON, SLOTS), 0, OT + 1), jax.random.fold_in(arg_keys[2], 1), 0, OT).astype(jnp.int32)
    remap_weight = noise(arg_keys[3], (N_LAT * SLOTS, TW, TW * N_LON), TW ** -0.5, 0.5, ((0, 8), (2, 4)))
    tracer = noise(arg_keys[4], (LEV, NY, NX), 1.0, 6.0, ((1, 8), (2, 4)), jnp.float32)
    diffusivity = jnp.clip(jnp.exp(math.log(0.12) - 1.7917595 * jax.random.uniform(arg_keys[5], (NY, NX), jnp.float32) ** level_of(arg_keys[5], (NY, NX), ((0, 8), (1, 4)), -0.2, 0.2)), 0.02, 0.12)
    zonal_velocity = jnp.clip(jax.random.uniform(arg_keys[6], (NY, NX), jnp.float32, -0.25, 0.25) * level_of(arg_keys[6], (NY, NX), ((0, 8), (1, 4)), -0.4, 0.0), -0.25, 0.25)
    merid_velocity = jnp.clip(jax.random.uniform(arg_keys[7], (NY, NX), jnp.float32, -0.25, 0.25) * level_of(arg_keys[7], (NY, NX), ((0, 8), (1, 4)), -0.4, 0.0), -0.25, 0.25)
    ocean_mask = plant((jax.random.randint(arg_keys[8], (NY, NX), 0, 5) < 4).astype(jnp.int32), jax.random.fold_in(arg_keys[8], 1), 0, 1)
    level_proj = noise(arg_keys[9], (LEV, NF), NF ** -0.5, 2.0, (), jnp.float32)
    return {"atm_flux": atm_flux, "send_tile": send_tile, "recv_tile": recv_tile, "remap_weight": remap_weight, "tracer": tracer, "diffusivity": diffusivity, "zonal_velocity": zonal_velocity, "merid_velocity": merid_velocity, "ocean_mask": ocean_mask, "level_proj": level_proj}


def advance(tracer_in, statics):
    diffuse = statics[0]
    zonal_vel = statics[1]
    merid_vel = statics[2]
    wet_cells = statics[3]
    face_wet = wet_cells[:, :-1] * wet_cells[:, 1:]
    face_vel = 0.5 * (zonal_vel[:, :-1] + zonal_vel[:, 1:]) * face_wet
    face_diff = 0.5 * (diffuse[:, :-1] + diffuse[:, 1:]) * face_wet
    left_cells = tracer_in[:, :, :-1]
    right_cells = tracer_in[:, :, 1:]
    flux_x = jnp.maximum(face_vel, 0.0) * left_cells + jnp.minimum(face_vel, 0.0) * right_cells - face_diff * (right_cells - left_cells)
    north_wet = wet_cells[:-1, :] * wet_cells[1:, :]
    north_vel = 0.5 * (merid_vel[:-1, :] + merid_vel[1:, :]) * north_wet
    north_diff = 0.5 * (diffuse[:-1, :] + diffuse[1:, :]) * north_wet
    lower_cells = tracer_in[:, :-1, :]
    upper_cells = tracer_in[:, 1:, :]
    flux_y = jnp.maximum(north_vel, 0.0) * lower_cells + jnp.minimum(north_vel, 0.0) * upper_cells - north_diff * (upper_cells - lower_cells)
    diverge = (flux_x[:, 1:-1, 1:] - flux_x[:, 1:-1, :-1]) + (flux_y[:, 1:, 1:-1] - flux_y[:, :-1, 1:-1])
    return tracer_in[:, 1:-1, 1:-1] - wet_cells[1:-1, 1:-1] * diverge


def extend(values, halo_depth, signs):
    zonal = jnp.concatenate([values[..., -halo_depth:], values, values[..., :halo_depth]], axis=-1)
    northern = zonal[:, -halo_depth:, :][:, ::-1, ::-1] * signs
    southern = jnp.zeros_like(northern)
    return jnp.concatenate([southern, zonal, northern], axis=1)


def reference(atm_flux, send_tile, recv_tile, remap_weight, tracer, diffusivity, zonal_velocity, merid_velocity, ocean_mask, level_proj):
    nearby = 2 * REACH + 1
    band_ids = jnp.arange(N_LAT, dtype=jnp.int32)[:, None]
    offset_ids = jnp.arange(nearby, dtype=jnp.int32)[None, :]
    sources = band_ids + REACH - offset_ids
    inside = (sources >= 0) & (sources < N_LAT)
    clipped = jnp.clip(sources, 0, N_LAT - 1).astype(jnp.int32)

    def column(block):
        atm_col = lax.dynamic_slice_in_dim(atm_flux, block * TW, TW, 3)
        lists = lax.dynamic_index_in_dim(send_tile, block, 1, keepdims=False).reshape(N_LAT, nearby, CAP)
        picked = lists[clipped, jnp.broadcast_to(offset_ids, clipped.shape)]
        tiles_in = atm_col[clipped[:, :, None], picked].astype(jnp.float32)
        tiles_in = jnp.where(inside[:, :, None, None, None], tiles_in, 0.0)
        weights_in = lax.dynamic_slice_in_dim(remap_weight, block * TW, TW, 2).reshape(N_LAT, nearby, CAP, TW, TW)
        contrib = jnp.einsum('rdcoa,rdcfa->rdcfo', weights_in.astype(jnp.float32), tiles_in)
        contrib = contrib.reshape(N_LAT, SLOTS, NF * TW)
        dests = lax.dynamic_index_in_dim(recv_tile, block, 1, keepdims=False)
        summed = jax.vmap(lambda values, ids: jax.ops.segment_sum(values, ids, num_segments=OT + 1))(contrib, dests)
        summed = summed[:, :OT].reshape(N_LAT, OY, OX // TW, NF, TW)
        return summed.transpose(3, 0, 1, 2, 4).reshape(NF, NY, OX)

    stacks = lax.map(column, jnp.arange(N_LON, dtype=jnp.int32))
    ocean_flux = stacks.transpose(1, 2, 0, 3).reshape(NF, NY, NX)
    current = tracer + jnp.einsum('lf,fyx->lyx', level_proj, ocean_flux, precision=lax.Precision.HIGHEST)
    statics = jnp.stack([diffusivity, zonal_velocity, merid_velocity, ocean_mask.astype(jnp.float32)])
    signs = jnp.array([1.0, -1.0, -1.0, 1.0], dtype=jnp.float32)[:, None, None]
    unit_sign = jnp.ones((1, 1, 1), dtype=jnp.float32)
    for step_index in range(STEPS):
        current = advance(extend(current, 1, unit_sign), extend(statics, 1, signs))
    return ocean_flux, current
```

```python
import functools

import jax
import jax.numpy as jnp
from jax import lax
from jax.experimental import pallas as pl
from jax.experimental.pallas import tpu as pltpu
from jax.sharding import PartitionSpec as P

CAP = 2
REACH = 2
STEPS = 4
LANES = 128
SUB = 8

VM = pl.BlockSpec(memory_space=pltpu.VMEM)
SM = pl.BlockSpec(memory_space=pltpu.SMEM)


def call(kernel, outs, in_specs, name, scratch=(), aliases=None, limit=12):
    return pl.pallas_call(
        kernel,
        out_shape=[jax.ShapeDtypeStruct(s, d) for s, d in outs],
        in_specs=in_specs,
        out_specs=[VM] * len(outs),
        scratch_shapes=list(scratch),
        input_output_aliases=aliases or {},
        compiler_params=pltpu.CompilerParams(vmem_limit_bytes=limit << 20),
        name=name,
    )


def swaps(pairs):
    return [route for a, b in pairs for route in ((a, b), (b, a))]


def band_parity():
    band = lax.axis_index("lat")
    return lax.rem(band, 2), lax.rem(lax.div(band, 2), 2)


def gather_kernel(send, atm, near, far, own):
    for target, base, d in ((near, 0, 1), (near, 2, 3), (far, 0, 0), (far, 2, 4), (own, 0, 2)):
        for c in range(CAP):
            target[base + c] = atm[0, send[0, 0, d * CAP + c]]


def relay_kernel(far, near, first, second):
    _, odd_pair = band_parity()
    a = CAP * (1 - odd_pair)
    b = CAP * odd_pair
    first[0:CAP] = far[pl.ds(a, CAP)]
    first[CAP : 2 * CAP] = near[pl.ds(a, CAP)]
    second[0:CAP] = far[pl.ds(b, CAP)]
    second[CAP : 2 * CAP] = near[pl.ds(b, CAP)]


def prepare_kernel(tracer, diff, zonal, merid, mask, rows_out, top, bottom):
    levels, rows, _ = tracer.shape
    for y in range(0, rows, SUB):
        for l in range(0, levels, SUB):
            block = tracer[l : l + SUB, y : y + SUB, :]
            rows_out[y : y + SUB, l : l + SUB, :] = jnp.swapaxes(block, 0, 1)
    for f, field in enumerate((diff, zonal, merid, mask)):
        low = field[0:STEPS, :].astype(jnp.float32)
        high = field[rows - STEPS : rows, :].astype(jnp.float32)
        bottom[f * STEPS : (f + 1) * STEPS, :] = low
        top[f * STEPS : (f + 1) * STEPS, :] = high


def remap_kernel(
    recv, own, near, first, second, weight, proj, start, top, bottom,
    forced, contrib, here, there, tiles,
):
    rows, levels, cols = forced.shape
    width = weight.shape[1]
    across = cols // width
    odd_core, odd_pair = band_parity()
    tiles[2 * CAP : 3 * CAP] = own[...]

    def place(above, below):
        tiles[0:CAP] = above[0:CAP]
        tiles[4 * CAP : 5 * CAP] = below[0:CAP]

        @pl.when(odd_core == 0)
        def _():
            tiles[CAP : 2 * CAP] = near[0:CAP]
            tiles[3 * CAP : 4 * CAP] = below[CAP : 2 * CAP]

        @pl.when(odd_core == 1)
        def _():
            tiles[CAP : 2 * CAP] = above[CAP : 2 * CAP]
            tiles[3 * CAP : 4 * CAP] = near[CAP : 2 * CAP]

    @pl.when(odd_pair == 0)
    def _():
        place(first, second)

    @pl.when(odd_pair == 1)
    def _():
        place(second, first)

    share = [jnp.broadcast_to(proj[:, f : f + 1], (levels, width)) for f in range(proj.shape[1])]
    for s in range(weight.shape[0]):
        part = lax.dot_general(
            tiles[s], weight[s], (((1,), (1,)), ((), ())), preferred_element_type=jnp.float32
        )
        contrib[s] = part
        update = share[0] * part[0:1, :]
        for f in range(1, proj.shape[1]):
            update = update + share[f] * part[f : f + 1, :]
        t = recv[0, 0, s]
        y = jnp.minimum(lax.div(t, across), rows - 1)
        at = pl.ds(pl.multiple_of(lax.rem(t, across) * width, width), width)
        update = jnp.where(t < rows * across, update, 0.0)
        forced[y, :, at] = forced[y, :, at] + update

    @pl.when(odd_core == 0)
    def _():
        here[0:STEPS] = forced[rows - STEPS : rows]
        here[STEPS] = top[...]
        there[0:STEPS] = forced[0:STEPS]
        there[STEPS] = bottom[...]

    @pl.when(odd_core == 1)
    def _():
        here[0:STEPS] = forced[0:STEPS]
        here[STEPS] = bottom[...]
        there[0:STEPS] = forced[rows - STEPS : rows]
        there[STEPS] = top[...]


def flux_kernel(recv, contrib, flux, landed):
    fields, rows, cols = flux.shape
    width = contrib.shape[2]
    across = cols // width
    landed[...] = jnp.zeros_like(landed)
    for s in range(contrib.shape[0]):
        t = recv[0, 0, s]
        y = jnp.minimum(lax.div(t, across), rows - 1)
        k = lax.rem(t, across)
        part = jnp.where(t < rows * across, contrib[s], 0.0)
        landed[k, y] = landed[k, y] + part
    for k in range(across):
        for y in range(0, rows, SUB):
            block = jnp.swapaxes(landed[k, y : y + SUB], 0, 1)
            flux[:, y : y + SUB, k * width : (k + 1) * width] = block


def lane_reversed(x):
    tiles = []
    for k in range(x.shape[-1] // LANES - 1, -1, -1):
        block = x[:, k * LANES : (k + 1) * LANES]
        index = LANES - 1 - lax.broadcasted_iota(jnp.int32, block.shape, 1)
        tiles.append(jnp.take_along_axis(block, index, axis=1))
    return tiles


SIGNS = (1.0, -1.0, -1.0, 1.0)


def pack_kernel(top_band, forced, here, there, diff, zonal, merid, mask, halo, static_halo, edges):
    rows, levels, cols = forced.shape
    odd_core, _ = band_parity()
    fold = lax.axis_index("lat") == top_band - 1

    def static_rows(base, part):
        for f in range(4):
            static_halo[f, base : base + STEPS, :] = part[STEPS, f * STEPS : (f + 1) * STEPS, :]

    def straight(base, part):
        halo[base : base + STEPS] = part[0:STEPS]
        static_rows(base, part)

    def folded(part):
        for i in range(STEPS):
            for l in range(0, levels, SUB):
                for n, block in enumerate(lane_reversed(part[STEPS - 1 - i, l : l + SUB, :])):
                    halo[i, l : l + SUB, n * LANES : (n + 1) * LANES] = block
        for r in range(0, 4 * STEPS, SUB):
            for n, block in enumerate(lane_reversed(part[STEPS, r : r + SUB, :])):
                for k in range(SUB):
                    f, i = divmod(r + k, STEPS)
                    static_halo[
                        f, STEPS - 1 - i : STEPS - i, n * LANES : (n + 1) * LANES
                    ] = SIGNS[f] * block[k : k + 1, :]

    @pl.when(odd_core == 0)
    def _():
        straight(0, here)
        straight(STEPS, there)

    @pl.when(odd_core == 1)
    def _():
        straight(STEPS, here)

        @pl.when(fold)
        def _():
            folded(there)

        @pl.when(jnp.logical_not(fold))
        def _():
            straight(0, there)

    lane = lax.broadcasted_iota(jnp.int32, (1, LANES), 1)
    group = lax.div(lax.rem(lane + 4, LANES), 8)
    left = lane < LANES // 2

    def both(row):
        return jnp.where(left, row[:, 0:LANES], row[:, cols - LANES : cols])

    per = LANES // 8
    for g in range((rows + 2 * STEPS + per - 1) // per):
        packed = jnp.zeros((levels, LANES), jnp.float32)
        for i in range(per):
            y = g * per + i
            if y >= rows + 2 * STEPS:
                break
            row = both(forced[y] if y < rows else halo[y - rows])
            packed = jnp.where(group == i, pltpu.roll(row, 8 * i, 1) if i else row, packed)
        edges[g * levels : (g + 1) * levels, :] = packed
    base = ((rows + 2 * STEPS + per - 1) // per) * levels
    blocks = rows // SUB
    inner = jnp.zeros((SUB, LANES), jnp.float32)
    outer = jnp.zeros((SUB, LANES), jnp.float32)
    for f, field in enumerate((diff, zonal, merid, mask)):
        for b in range(blocks):
            i = f * blocks + b
            row = both(field[b * SUB : (b + 1) * SUB, :].astype(jnp.float32))
            inner = jnp.where(group == i, pltpu.roll(row, 8 * i, 1) if i else row, inner)
        row = both(static_halo[f])
        outer = jnp.where(group == f, pltpu.roll(row, 8 * f, 1) if f else row, outer)
    edges[base : base + SUB, :] = inner
    edges[base + SUB : base + 2 * SUB, :] = outer


def step_kernel(
    forced, halo, diff, zonal, merid, mask, static_halo, first, second, out, now, later, coef,
):
    rows, levels, cols = forced.shape
    wide = cols + LANES
    tall = rows + 2 * STEPS
    odd_block = lax.rem(lax.axis_index("lon"), 2)
    lane = lax.broadcasted_iota(jnp.int32, first.shape, 1)
    from_east = (lax.rem(lane, 8) < 4) == (odd_block == 0)
    edges = jnp.where(from_east, first[...], second[...])
    per = LANES // 8
    for y in range(tall):
        n = y + STEPS if y < rows + STEPS else y - rows - STEPS
        now[n, :, 0:cols] = forced[y] if y < rows else halo[y - rows]
        g, i = y // per, y % per
        side = edges[g * levels : (g + 1) * levels, :]
        now[n, :, cols:wide] = pltpu.roll(side, LANES - 8 * i, 1) if i else side

    base = ((tall + per - 1) // per) * levels
    blocks = rows // SUB
    inner = edges[base : base + SUB, :]
    outer = edges[base + SUB : base + 2 * SUB, :]
    fields = []
    for f, field in enumerate((diff, zonal, merid, mask)):
        columns = []
        for b in range(blocks):
            i = f * blocks + b
            columns.append(pltpu.roll(inner, LANES - 8 * i, 1) if i else inner)
        columns.append(pltpu.roll(outer, LANES - 8 * f, 1) if f else outer)
        body = jnp.concatenate([field[...].astype(jnp.float32), static_halo[f]], axis=0)
        fields.append(jnp.concatenate([body, jnp.concatenate(columns, axis=0)], axis=1))
    d, u, v, wet = fields

    def east(x):
        return pltpu.roll(x, wide - 1, 1)

    def west(x):
        return pltpu.roll(x, 1, 1)

    def north(x):
        return jnp.concatenate([x[1:], x[:1]], axis=0)

    def south(x):
        return jnp.concatenate([x[-1:], x[:-1]], axis=0)

    def face(vel, shift):
        w = wet * shift(wet)
        speed = 0.5 * (vel + shift(vel)) * w
        mix = 0.5 * (d + shift(d)) * w
        return jnp.maximum(speed, 0.0) + mix, jnp.minimum(speed, 0.0) - mix

    ae, be = face(u, east)
    an, bn = face(v, north)
    aw, bw = west(ae), west(be)
    az, bz = south(an), south(bn)
    center = 1.0 - wet * (ae - bw + an - bz)
    for k, value in enumerate((center, -wet * be, wet * aw, -wet * bn, wet * az)):
        coef[k, 0:STEPS, :] = value[tall - STEPS : tall]
        coef[k, STEPS : tall - STEPS, :] = value[0 : tall - 2 * STEPS]
        coef[k, tall - STEPS : tall, :] = value[tall - 2 * STEPS : tall - STEPS]

    def updated(src, n):
        c = src[n]
        k = [jnp.broadcast_to(coef[m, pl.ds(n, 1), :], (levels, wide)) for m in range(5)]
        return (
            k[0] * c + k[1] * east(c) + k[2] * west(c) + k[3] * src[n + 1] + k[4] * src[n - 1]
        )

    src, dst = now, later
    for step in range(1, STEPS):
        def row(n, carry, src=src, dst=dst):
            dst[n] = updated(src, n)
            return carry

        lax.fori_loop(step, tall - step, row, 0, unroll=2)
        src, dst = dst, src

    def rows_of(b, carry):
        first_row = pl.multiple_of(b * SUB, SUB)
        block = jnp.stack([updated(src, STEPS + first_row + i)[:, 0:cols] for i in range(SUB)])
        for l in range(0, levels, SUB):
            out[l : l + SUB, pl.ds(first_row, SUB), :] = jnp.swapaxes(block[:, l : l + SUB], 0, 1)
        return carry

    lax.fori_loop(0, rows // SUB, rows_of, 0)


def body(
    atm_flux,
    send_tile,
    recv_tile,
    remap_weight,
    tracer,
    diffusivity,
    zonal_velocity,
    merid_velocity,
    ocean_mask,
    level_proj,
):
    bands, blocks = lax.axis_size("lat"), lax.axis_size("lon")
    fields, width = atm_flux.shape[2:]
    levels, rows, cols = tracer.shape
    slots = remap_weight.shape[0]
    f32, bf16 = jnp.float32, jnp.bfloat16
    statics = (diffusivity, zonal_velocity, merid_velocity, ocean_mask)
    tile4 = ((2 * CAP, fields, width), bf16)

    core_pairs = swaps([(i, i + 1) for i in range(0, bands, 2)])
    chips = [(i, i + 1) for i in range(bands // 2 - 1)]
    even_chips = swaps([(2 * a + k, 2 * b + k) for a, b in chips[0::2] for k in (0, 1)])
    odd_chips = swaps([(2 * a + k, 2 * b + k) for a, b in chips[1::2] for k in (0, 1)])
    last = (bands - 1) * blocks
    across_chips = swaps(
        [(i * blocks + j, (i + 1) * blocks + j) for i in range(1, bands - 1, 2) for j in range(blocks)]
    ) + [(last + j, last + blocks - 1 - j) for j in range(blocks)]
    even_blocks = swaps([(j, j + 1) for j in range(0, blocks, 2)])
    odd_blocks = swaps([(j, (j + 1) % blocks) for j in range(1, blocks, 2)])

    near, far, own = call(
        gather_kernel, [tile4, tile4, ((CAP, fields, width), bf16)], [SM, VM], "gather"
    )(send_tile, atm_flux)
    near_in = lax.ppermute(near, "lat", core_pairs)
    first, second = call(relay_kernel, [tile4, tile4], [VM, VM], "relay")(far, near_in)
    first = lax.ppermute(first, "lat", even_chips)
    second = lax.ppermute(second, "lat", odd_chips)
    start, top, bottom = call(
        prepare_kernel,
        [((rows, levels, cols), f32), ((4 * STEPS, cols), f32), ((4 * STEPS, cols), f32)],
        [VM] * 5,
        "prepare",
    )(tracer, *statics)
    ring = ((STEPS + 1, levels, cols), f32)
    forced, contrib, here, there = call(
        remap_kernel,
        [((rows, levels, cols), f32), ((slots, fields, width), f32), ring, ring],
        [SM] + [VM] * 9,
        "remap",
        scratch=[pltpu.VMEM((slots, fields, width), bf16)],
        aliases={7: 0},
    )(recv_tile, own, near_in, first, second, remap_weight, level_proj, start, top, bottom)
    here = lax.ppermute(here, "lat", core_pairs)
    there = lax.ppermute(there, ("lat", "lon"), across_chips)
    (ocean_flux,) = call(
        flux_kernel,
        [((fields, rows, cols), f32)],
        [SM, VM],
        "flux",
        scratch=[pltpu.VMEM((cols // width, rows, fields, width), f32)],
    )(recv_tile, contrib)
    per = LANES // 8
    packed_rows = ((rows + 2 * STEPS + per - 1) // per) * levels + 2 * SUB
    halo, static_halo, edges = call(
        functools.partial(pack_kernel, bands),
        [((2 * STEPS, levels, cols), f32), ((4, 2 * STEPS, cols), f32), ((packed_rows, LANES), f32)],
        [VM] * 7,
        "pack",
    )(forced, here, there, *statics)
    first = lax.ppermute(edges, "lon", even_blocks)
    second = lax.ppermute(edges, "lon", odd_blocks)
    tall, wide = rows + 2 * STEPS, cols + LANES
    (out,) = call(
        step_kernel,
        [((levels, rows, cols), f32)],
        [VM] * 9,
        "steps",
        scratch=[
            pltpu.VMEM((tall, levels, wide), f32),
            pltpu.VMEM((tall, levels, wide), f32),
            pltpu.VMEM((5, tall, wide), f32),
        ],
    )(forced, halo, *statics, static_halo, first, second)
    return (ocean_flux, out)


def solution(mesh):
    placed = (
        P("lat", None, None, "lon"),
        P("lat", "lon", None),
        P("lat", "lon", None),
        P("lat", None, "lon"),
        P(None, "lat", "lon"),
        P("lat", "lon"),
        P("lat", "lon"),
        P("lat", "lon"),
        P("lat", "lon"),
        P(),
    )
    return jax.shard_map(
        body,
        mesh=mesh,
        in_specs=placed,
        out_specs=(P(None, "lat", "lon"), P(None, "lat", "lon")),
        check_vma=False,
    )
```

```python
import functools

import jax
import jax.numpy as jnp
from jax import lax
from jax.experimental import pallas as pl
from jax.experimental.pallas import tpu as pltpu
from jax.sharding import PartitionSpec as P

CAP = 2
REACH = 2
STEPS = 4
LANES = 128
SUB = 8

VM = pl.BlockSpec(memory_space=pltpu.VMEM)
SM = pl.BlockSpec(memory_space=pltpu.SMEM)
HB = pl.BlockSpec(memory_space=pltpu.HBM)


def call(kernel, outs, in_specs, name, scratch=(), aliases=None, limit=12, out_specs=None):
    return pl.pallas_call(
        kernel,
        out_shape=[jax.ShapeDtypeStruct(s, d) for s, d in outs],
        in_specs=in_specs,
        out_specs=out_specs or [VM] * len(outs),
        scratch_shapes=list(scratch),
        input_output_aliases=aliases or {},
        compiler_params=pltpu.CompilerParams(vmem_limit_bytes=limit << 20),
        name=name,
    )


def in_hbm(*arrays):
    return [pltpu.with_memory_space_constraint(x, pltpu.HBM) for x in arrays]


def swaps(pairs):
    return [route for a, b in pairs for route in ((a, b), (b, a))]


def band_parity():
    band = lax.axis_index("lat")
    return lax.rem(band, 2), lax.rem(lax.div(band, 2), 2)


def gather_kernel(send_hbm, atm_hbm, near, far, own, send, atm, sems):
    copies = [
        pltpu.make_async_copy(send_hbm, send, sems.at[0]),
        pltpu.make_async_copy(atm_hbm, atm, sems.at[1]),
    ]
    for copy in copies:
        copy.start()
    for copy in copies:
        copy.wait()
    for target, base, d in ((near, 0, 1), (near, 2, 3), (far, 0, 0), (far, 2, 4), (own, 0, 2)):
        for c in range(CAP):
            target[base + c] = atm[0, send[0, 0, d * CAP + c]]


def relay_kernel(far, near, first, second):
    _, odd_pair = band_parity()
    a = CAP * (1 - odd_pair)
    b = CAP * odd_pair
    first[0:CAP] = far[pl.ds(a, CAP)]
    first[CAP : 2 * CAP] = near[pl.ds(a, CAP)]
    second[0:CAP] = far[pl.ds(b, CAP)]
    second[CAP : 2 * CAP] = near[pl.ds(b, CAP)]


def faces(vel, d, wet, vel_next, d_next, wet_next):
    w = wet * wet_next
    speed = 0.5 * (vel + vel_next) * w
    mix = 0.5 * (d + d_next) * w
    return jnp.maximum(speed, 0.0) + mix, jnp.minimum(speed, 0.0) - mix


def stencil(wet, east, west, north, south):
    center = 1.0 - wet * (east[0] - west[1] + north[0] - south[1])
    return center, -wet * east[1], wet * west[0], -wet * north[1], wet * south[0]


def band_stencil(fields):
    d, u, v, wet = fields
    cols = d.shape[1]

    def moved(x, by, axis):
        if axis:
            return pltpu.roll(x, by % cols, 1)
        return jnp.concatenate([x[-by:], x[:-by]], axis=0)

    east = faces(u, d, wet, *(moved(x, -1, 1) for x in (u, d, wet)))
    north = faces(v, d, wet, *(moved(x, -1, 0) for x in (v, d, wet)))
    west = tuple(moved(x, 1, 1) for x in east)
    south = tuple(moved(x, 1, 0) for x in north)
    return stencil(wet, east, west, north, south)


def run_band(size, read, coef, base, buffers, pre, target):
    levels, _, cols = pre.shape
    src = read
    for step in range(1, STEPS + 1):
        new = []
        for n in range(step, size - step):
            c = src(n)
            k = [
                jnp.broadcast_to(coef[m, base + n : base + n + 1, :], (levels, cols))
                for m in range(5)
            ]
            value = (
                k[0] * c
                + k[1] * pltpu.roll(c, cols - 1, 1)
                + k[2] * pltpu.roll(c, 1, 1)
                + k[3] * src(n + 1)
                + k[4] * src(n - 1)
            )
            if step < STEPS:
                buffers[step % 2, n] = value
            else:
                new.append(value)
                if len(new) == SUB:
                    block = jnp.stack(new)
                    at = target + n - STEPS - SUB + 1
                    for l in range(0, levels, SUB):
                        pre[l : l + SUB, at : at + SUB, :] = jnp.swapaxes(
                            block[:, l : l + SUB], 0, 1
                        )
                    new = []
        src = lambda n, held=buffers.at[step % 2]: held[n]


def prepare_kernel(
    tracer_hbm, diff_hbm, zonal_hbm, merid_hbm, mask_hbm, weight_hbm, proj_hbm, recv_hbm,
    rows_out, across, top, bottom, fields, coef, weight, share, recv,
    tracer, mask, proj, sems,
):
    levels, rows, cols = tracer.shape
    sources = (tracer_hbm, diff_hbm, zonal_hbm, merid_hbm, mask_hbm, proj_hbm, weight_hbm, recv_hbm)
    targets = (tracer, fields.at[0], fields.at[1], fields.at[2], mask, proj, weight, recv)
    copies = [pltpu.make_async_copy(a, b, sems.at[k]) for k, (a, b) in enumerate(zip(sources, targets))]
    for copy in copies:
        copy.start()
    for copy in copies[1:6]:
        copy.wait()
    fields[3] = mask[...].astype(jnp.float32)
    for f in range(share.shape[0]):
        share[f] = jnp.broadcast_to(jnp.swapaxes(proj[f : f + 1, :], 0, 1), share.shape[1:])
    parts = [fields[f] for f in range(4)]
    zero = jnp.zeros((SUB, cols), jnp.float32)
    for y in range(0, rows, SUB):
        stacked = jnp.stack([x[y : y + SUB] for x in parts] + [zero] * (SUB - 4))
        across[y : y + SUB] = jnp.swapaxes(stacked, 0, 1)
    for f, x in enumerate(parts):
        bottom[f * STEPS : (f + 1) * STEPS, :] = x[0:STEPS]
        top[f * STEPS : (f + 1) * STEPS, :] = x[rows - STEPS : rows]
    for m, value in enumerate(band_stencil(parts)):
        coef[m] = value
    copies[0].wait()
    for y in range(0, rows, SUB):
        for l in range(0, levels, SUB):
            block = tracer[l : l + SUB, y : y + SUB, :]
            rows_out[y : y + SUB, l : l + SUB, :] = jnp.swapaxes(block, 0, 1)
    copies[6].wait()
    copies[7].wait()


def remap_kernel(
    recv, own, near, first, second, weight, share, start, top, bottom,
    forced, contrib, here, there, tiles,
):
    rows, levels, cols = forced.shape
    width = weight.shape[1]
    across = cols // width
    odd_core, odd_pair = band_parity()
    tiles[2 * CAP : 3 * CAP] = own[...]

    def place(above, below):
        tiles[0:CAP] = above[0:CAP]
        tiles[4 * CAP : 5 * CAP] = below[0:CAP]

        @pl.when(odd_core == 0)
        def _():
            tiles[CAP : 2 * CAP] = near[0:CAP]
            tiles[3 * CAP : 4 * CAP] = below[CAP : 2 * CAP]

        @pl.when(odd_core == 1)
        def _():
            tiles[CAP : 2 * CAP] = above[CAP : 2 * CAP]
            tiles[3 * CAP : 4 * CAP] = near[CAP : 2 * CAP]

    @pl.when(odd_pair == 0)
    def _():
        place(first, second)

    @pl.when(odd_pair == 1)
    def _():
        place(second, first)

    for s in range(weight.shape[0]):
        part = lax.dot_general(
            tiles[s], weight[s], (((1,), (1,)), ((), ())), preferred_element_type=jnp.float32
        )
        contrib[s] = part
        update = share[0] * part[0:1, :]
        for f in range(1, share.shape[0]):
            update = update + share[f] * part[f : f + 1, :]
        t = recv[0, 0, s]
        y = jnp.minimum(lax.div(t, across), rows - 1)
        at = pl.ds(pl.multiple_of(lax.rem(t, across) * width, width), width)
        update = jnp.where(t < rows * across, update, 0.0)
        forced[y, :, at] = forced[y, :, at] + update

    @pl.when(odd_core == 0)
    def _():
        here[0:STEPS] = forced[rows - STEPS : rows]
        here[STEPS] = top[...]
        there[0:STEPS] = forced[0:STEPS]
        there[STEPS] = bottom[...]

    @pl.when(odd_core == 1)
    def _():
        here[0:STEPS] = forced[0:STEPS]
        here[STEPS] = bottom[...]
        there[0:STEPS] = forced[rows - STEPS : rows]
        there[STEPS] = top[...]


def flux_kernel(recv, contrib, flux, landed):
    fields, rows, cols = flux.shape
    width = contrib.shape[2]
    across = cols // width
    landed[...] = jnp.zeros_like(landed)
    for s in range(contrib.shape[0]):
        t = recv[0, 0, s]
        y = jnp.minimum(lax.div(t, across), rows - 1)
        k = lax.rem(t, across)
        part = jnp.where(t < rows * across, contrib[s], 0.0)
        landed[k, y] = landed[k, y] + part
    for k in range(across):
        for y in range(0, rows, SUB):
            block = jnp.swapaxes(landed[k, y : y + SUB], 0, 1)
            flux[:, y : y + SUB, k * width : (k + 1) * width] = block


def slot_masks(slots):
    wide = LANES // slots
    lane = lax.broadcasted_iota(jnp.int32, (1, LANES), 1)
    slot = lax.rem(lax.div(lane + wide // 2, wide), slots)
    place = lax.rem(lane + wide // 2, wide)
    return lane, slot, place, wide


def rolled(x, by):
    by = by % LANES
    return pltpu.roll(x, by, 1) if by else x


def slotted(row, i, wide, place):
    first = rolled(row[:, 0:LANES], wide * i + STEPS)
    last = rolled(row[:, row.shape[1] - LANES :], wide * i - STEPS)
    return jnp.where(place < wide // 2, last, first)


def inside_kernel(forced, across, coef, pre, packed, buffers):
    rows, levels, cols = forced.shape
    slots = rows // SUB
    _, slot, place, wide = slot_masks(slots)
    for part, base in ((forced, 0), (across, levels)):
        for l in range(0, part.shape[1], SUB):
            for q in range(SUB):
                tile = None
                for i in range(slots):
                    piece = slotted(part[SUB * i + q, l : l + SUB, :], i, wide, place)
                    tile = piece if tile is None else jnp.where(slot == i, piece, tile)
                packed[q, base + l : base + l + SUB, :] = tile
    size = rows - 2 * (SUB - STEPS)
    run_band(size, lambda n: forced[SUB - STEPS + n], coef, SUB - STEPS, buffers, pre, SUB)


def lane_reversed(x):
    tiles = []
    for k in range(x.shape[-1] // LANES - 1, -1, -1):
        block = x[:, k * LANES : (k + 1) * LANES]
        index = LANES - 1 - lax.broadcasted_iota(jnp.int32, block.shape, 1)
        tiles.append(jnp.take_along_axis(block, index, axis=1))
    return tiles


SIGNS = (1.0, -1.0, -1.0, 1.0)


def pack_kernel(top_band, here, there, packed, halo, static_halo, outer, edges):
    levels, cols = halo.shape[1:]
    odd_core, _ = band_parity()
    fold = lax.axis_index("lat") == top_band - 1

    def straight(base, part):
        halo[base : base + STEPS] = part[0:STEPS]
        for f in range(4):
            static_halo[f, base : base + STEPS, :] = part[STEPS, f * STEPS : (f + 1) * STEPS, :]

    def folded(part):
        for i in range(STEPS):
            for l in range(0, levels, SUB):
                for n, block in enumerate(lane_reversed(part[STEPS - 1 - i, l : l + SUB, :])):
                    halo[i, l : l + SUB, n * LANES : (n + 1) * LANES] = block
        for r in range(0, 4 * STEPS, SUB):
            for n, block in enumerate(lane_reversed(part[STEPS, r : r + SUB, :])):
                for k in range(SUB):
                    f, i = divmod(r + k, STEPS)
                    static_halo[
                        f, STEPS - 1 - i : STEPS - i, n * LANES : (n + 1) * LANES
                    ] = SIGNS[f] * block[k : k + 1, :]

    @pl.when(odd_core == 0)
    def _():
        straight(0, here)
        straight(STEPS, there)

    @pl.when(odd_core == 1)
    def _():
        straight(STEPS, here)

        @pl.when(fold)
        def _():
            folded(there)

        @pl.when(jnp.logical_not(fold))
        def _():
            straight(0, there)

    slots = packed.shape[0] // 2
    lane, slot, place, wide = slot_masks(slots)
    zero = jnp.zeros((SUB, cols), jnp.float32)
    stacked = jnp.stack([static_halo[f] for f in range(4)] + [zero] * (SUB - 4))
    statics = jnp.swapaxes(stacked, 0, 1)
    for m in range(STEPS):
        for l in range(0, levels + SUB, SUB):
            if l < levels:
                above, below = halo[m, l : l + SUB, :], halo[STEPS + m, l : l + SUB, :]
            else:
                above, below = statics[m], statics[STEPS + m]
            north = slotted(above, slots - 1, wide, place)
            south = slotted(below, 0, wide, place)
            outer[m, l : l + SUB, :] = jnp.where(slot == 0, south, north)

    turn = lax.div(lax.rem(lane, wide), 2 * STEPS)
    is_first = lax.rem(lane, 2 * STEPS) < STEPS
    per = wide // (2 * STEPS)
    for g in range(3):
        total = None
        for m in range(per):
            tile = packed[g * per + m] if g < 2 else outer[m]
            first = rolled(tile, 2 * STEPS * m - STEPS)
            last = rolled(tile, 2 * STEPS * m + 3 * STEPS)
            piece = jnp.where(is_first, first, last)
            total = piece if total is None else jnp.where(turn == m, piece, total)
        edges[g] = total


def bands_kernel(forced, halo, fields, static_halo, held, pre, coef, buffers):
    rows, levels, cols = forced.shape
    size = SUB + 2 * STEPS
    low = [
        jnp.concatenate([static_halo[f, STEPS : 2 * STEPS], fields[f, 0 : size - STEPS]], axis=0)
        for f in range(4)
    ]
    high = [
        jnp.concatenate([fields[f, rows - size + STEPS : rows], static_halo[f, 0:STEPS]], axis=0)
        for f in range(4)
    ]
    for b, parts in enumerate((low, high)):
        for m, value in enumerate(band_stencil(parts)):
            coef[m, b * size : (b + 1) * size, :] = value
    del held

    def low_row(n):
        return halo[STEPS + n] if n < STEPS else forced[n - STEPS]

    def high_row(n):
        y = rows - size + STEPS + n
        return forced[y] if y < rows else halo[y - rows]

    run_band(size, low_row, coef, 0, buffers.at[0], pre, 0)
    run_band(size, high_row, coef, size, buffers.at[1], pre, rows - SUB)


def edge_kernel(pre, packed, outer, first, second, out, tiles, coef, stage, sems):
    levels, rows, cols = pre.shape
    slots = rows // SUB
    lane, slot, place, wide = slot_masks(slots)
    odd_block = lax.rem(lax.axis_index("lon"), 2)
    per = wide // (2 * STEPS)
    from_east = (lax.rem(lane, 2 * STEPS) < STEPS) == (odd_block == 0)
    outside = jnp.abs(2 * place - (wide - 1)) < 2 * STEPS
    depth = levels + SUB
    count = SUB + 2 * STEPS
    for l in range(0, depth, SUB):
        at = slice(l, l + SUB)
        got = [jnp.where(from_east, first[g, at], second[g, at]) for g in range(3)]
        inner = []
        for q in range(SUB):
            halo = rolled(got[q // per], -(2 * STEPS * (q % per) + STEPS))
            inner.append(jnp.where(outside, halo, packed[q, at]))
        for m in range(STEPS):
            halo = rolled(got[2], -(2 * STEPS * m + STEPS))
            beyond = jnp.where(outside, halo, outer[m, at])
            tiles[0, STEPS + SUB + m, at] = jnp.where(
                slot == slots - 1, beyond, rolled(inner[m], -wide)
            )
            tiles[0, m, at] = jnp.where(slot == 0, beyond, rolled(inner[SUB - STEPS + m], wide))
        for q in range(SUB):
            tiles[0, STEPS + q, at] = inner[q]

    def static(n, f):
        return jnp.broadcast_to(tiles[0, n, levels + f : levels + f + 1, :], (SUB, LANES))

    below = None
    now = [static(0, f) for f in range(4)]
    for n in range(count - 1):
        after = [static(n + 1, f) for f in range(4)]
        d, u, v, wet = now
        north = faces(v, d, wet, after[2], after[0], after[3])
        if n:
            east = faces(u, d, wet, rolled(u, -1), rolled(d, -1), rolled(wet, -1))
            west = tuple(rolled(x, 1) for x in east)
            for m, value in enumerate(stencil(wet, east, west, north, below)):
                coef[m, n] = value
        below, now = north, after
    for step in range(1, STEPS + 1):
        src, dst = (step - 1) % 2, step % 2
        for n in range(step, count - step):
            k = [coef[m, n] for m in range(5)]
            for l in range(0, levels, SUB):
                at = slice(l, l + SUB)
                c = tiles[src, n, at]
                tiles[dst, n, at] = (
                    k[0] * c
                    + k[1] * rolled(c, -1)
                    + k[2] * rolled(c, 1)
                    + k[3] * tiles[src, n + 1, at]
                    + k[4] * tiles[src, n - 1, at]
                )
    final = STEPS % 2
    copies = []
    for l in range(0, levels, SUB):
        block = jnp.stack([tiles[final, STEPS + q, l : l + SUB] for q in range(SUB)])
        turned = jnp.swapaxes(block, 0, 1)
        for k in range(SUB):
            for i in range(slots):
                y = slice(i * SUB, (i + 1) * SUB)
                low = rolled(turned[k], -(wide * i + STEPS))
                high = rolled(turned[k], -(wide * i - STEPS))
                body = pre[l + k, y, :]
                stage[l + k, y, 0:LANES] = jnp.where(lane < STEPS, low, body[:, 0:LANES])
                for x in range(LANES, cols - LANES, LANES):
                    stage[l + k, y, x : x + LANES] = body[:, x : x + LANES]
                stage[l + k, y, cols - LANES : cols] = jnp.where(
                    lane >= LANES - STEPS, high, body[:, cols - LANES : cols]
                )
        copy = pltpu.make_async_copy(
            stage.at[l : l + SUB], out.at[l : l + SUB], sems.at[l // SUB]
        )
        copy.start()
        copies.append(copy)
    for copy in copies:
        copy.wait()


def body(
    atm_flux,
    send_tile,
    recv_tile,
    remap_weight,
    tracer,
    diffusivity,
    zonal_velocity,
    merid_velocity,
    ocean_mask,
    level_proj,
):
    bands, blocks = lax.axis_size("lat"), lax.axis_size("lon")
    fields, width = atm_flux.shape[2:]
    levels, rows, cols = tracer.shape
    slots = remap_weight.shape[0]
    f32, bf16 = jnp.float32, jnp.bfloat16
    statics = (diffusivity, zonal_velocity, merid_velocity, ocean_mask)
    tile4 = ((2 * CAP, fields, width), bf16)

    core_pairs = swaps([(i, i + 1) for i in range(0, bands, 2)])
    chips = [(i, i + 1) for i in range(bands // 2 - 1)]
    even_chips = swaps([(2 * a + k, 2 * b + k) for a, b in chips[0::2] for k in (0, 1)])
    odd_chips = swaps([(2 * a + k, 2 * b + k) for a, b in chips[1::2] for k in (0, 1)])
    last = (bands - 1) * blocks
    across_chips = swaps(
        [(i * blocks + j, (i + 1) * blocks + j) for i in range(1, bands - 1, 2) for j in range(blocks)]
    ) + [(last + j, last + blocks - 1 - j) for j in range(blocks)]
    even_blocks = swaps([(j, j + 1) for j in range(0, blocks, 2)])
    odd_blocks = swaps([(j, (j + 1) % blocks) for j in range(1, blocks, 2)])

    near, far, own = call(
        gather_kernel,
        [tile4, tile4, ((CAP, fields, width), bf16)],
        [HB, HB],
        "gather",
        scratch=[
            pltpu.SMEM(send_tile.shape, jnp.int32),
            pltpu.VMEM(atm_flux.shape, bf16),
            pltpu.SemaphoreType.DMA((2,)),
        ],
    )(*in_hbm(send_tile, atm_flux))
    near_in = lax.ppermute(near, "lat", core_pairs)
    first, second = call(relay_kernel, [tile4, tile4], [VM, VM], "relay")(far, near_in)
    first = lax.ppermute(first, "lat", even_chips)
    second = lax.ppermute(second, "lat", odd_chips)
    start, across, top, bottom, parts, coef, weight, share, recv = call(
        prepare_kernel,
        [
            ((rows, levels, cols), f32),
            ((rows, SUB, cols), f32),
            ((4 * STEPS, cols), f32),
            ((4 * STEPS, cols), f32),
            ((4, rows, cols), f32),
            ((5, rows, cols), f32),
            (remap_weight.shape, bf16),
            ((fields, levels, width), f32),
            (recv_tile.shape, jnp.int32),
        ],
        [HB] * 8,
        "prepare",
        scratch=[
            pltpu.VMEM(tracer.shape, f32),
            pltpu.VMEM((rows, cols), jnp.int32),
            pltpu.VMEM((fields, levels), f32),
            pltpu.SemaphoreType.DMA((8,)),
        ],
    )(*in_hbm(tracer, *statics, remap_weight, level_proj.T, recv_tile))
    ring = ((STEPS + 1, levels, cols), f32)
    forced, contrib, here, there = call(
        remap_kernel,
        [((rows, levels, cols), f32), ((slots, fields, width), f32), ring, ring],
        [SM] + [VM] * 9,
        "remap",
        scratch=[pltpu.VMEM((slots, fields, width), bf16)],
        aliases={7: 0},
    )(recv, own, near_in, first, second, weight, share, start, top, bottom)
    here = lax.ppermute(here, "lat", core_pairs)
    there = lax.ppermute(there, ("lat", "lon"), across_chips)
    (ocean_flux,) = call(
        flux_kernel,
        [((fields, rows, cols), f32)],
        [SM, VM],
        "flux",
        scratch=[pltpu.VMEM((cols // width, rows, fields, width), f32)],
    )(recv, contrib)
    depth = levels + SUB
    count = SUB + 2 * STEPS
    pre, packed = call(
        inside_kernel,
        [((levels, rows, cols), f32), ((SUB, depth, LANES), f32)],
        [VM] * 3,
        "inside",
        scratch=[pltpu.VMEM((2, rows, levels, cols), f32)],
    )(forced, across, coef)
    halo, static_halo, outer, edges = call(
        functools.partial(pack_kernel, bands),
        [
            ((2 * STEPS, levels, cols), f32),
            ((4, 2 * STEPS, cols), f32),
            ((STEPS, depth, LANES), f32),
            ((3, depth, LANES), f32),
        ],
        [VM] * 3,
        "pack",
    )(here, there, packed)
    first = lax.ppermute(edges, "lon", even_blocks)
    second = lax.ppermute(edges, "lon", odd_blocks)
    (pre,) = call(
        bands_kernel,
        [((levels, rows, cols), f32)],
        [VM] * 5,
        "bands",
        scratch=[
            pltpu.VMEM((5, 2 * count, cols), f32),
            pltpu.VMEM((2, 2, count, levels, cols), f32),
        ],
        aliases={4: 0},
    )(forced, halo, parts, static_halo, pre)
    (out,) = call(
        edge_kernel,
        [((levels, rows, cols), f32)],
        [VM] * 5,
        "edges",
        scratch=[
            pltpu.VMEM((2, count, depth, LANES), f32),
            pltpu.VMEM((5, count, SUB, LANES), f32),
            pltpu.VMEM((levels, rows, cols), f32),
            pltpu.SemaphoreType.DMA((levels // SUB,)),
        ],
        out_specs=[HB],
    )(pre, packed, outer, first, second)
    return (ocean_flux, out)


def solution(mesh):
    placed = (
        P("lat", None, None, "lon"),
        P("lat", "lon", None),
        P("lat", "lon", None),
        P("lat", None, "lon"),
        P(None, "lat", "lon"),
        P("lat", "lon"),
        P("lat", "lon"),
        P("lat", "lon"),
        P("lat", "lon"),
        P(),
    )
    return jax.shard_map(
        body,
        mesh=mesh,
        in_specs=placed,
        out_specs=(P(None, "lat", "lon"), P(None, "lat", "lon")),
        check_vma=False,
    )
```

```python
import functools

import jax
import jax.numpy as jnp
from jax import lax
from jax.experimental import pallas as pl
from jax.experimental.pallas import tpu as pltpu
from jax.sharding import PartitionSpec as P

CAP = 2
REACH = 2
STEPS = 4
LANES = 128
SUB = 8

VM = pl.BlockSpec(memory_space=pltpu.VMEM)
SM = pl.BlockSpec(memory_space=pltpu.SMEM)
HB = pl.BlockSpec(memory_space=pltpu.HBM)


def call(kernel, outs, in_specs, name, scratch=(), aliases=None, limit=12, out_specs=None):
    run = pl.pallas_call(
        kernel,
        out_shape=[jax.ShapeDtypeStruct(s, d) for s, d in outs],
        in_specs=in_specs,
        out_specs=out_specs or [VM] * len(outs),
        scratch_shapes=list(scratch),
        input_output_aliases=aliases or {},
        compiler_params=pltpu.CompilerParams(vmem_limit_bytes=limit << 20),
        name=name,
    )

    def scoped(*args):
        with jax.named_scope("run_" + name):
            return run(*args)

    return scoped


def in_hbm(*arrays):
    return [pltpu.with_memory_space_constraint(x, pltpu.HBM) for x in arrays]


def filled(routes, size):
    busy = {a for a, _ in routes}
    free = [i for i in range(size) if i not in busy]
    return routes + swaps(list(zip(free[0::2], free[1::2])))


def traded(x, axis, pairs, name):
    with jax.named_scope(name):
        return lax.ppermute(x, axis, pairs)


def swaps(pairs):
    return [route for a, b in pairs for route in ((a, b), (b, a))]


def band_parity():
    band = lax.axis_index("lat")
    return lax.rem(band, 2), lax.rem(lax.div(band, 2), 2)


def gather_kernel(send_hbm, atm_hbm, near, far, own, send, atm, sems):
    copies = [
        pltpu.make_async_copy(send_hbm, send, sems.at[0]),
        pltpu.make_async_copy(atm_hbm, atm, sems.at[1]),
    ]
    for copy in copies:
        copy.start()
    for copy in copies:
        copy.wait()
    for target, base, d in ((near, 0, 1), (near, 2, 3), (far, 0, 0), (far, 2, 4), (own, 0, 2)):
        for c in range(CAP):
            target[base + c] = atm[0, send[0, 0, d * CAP + c]]


def relay_kernel(far, near, first, second):
    _, odd_pair = band_parity()
    a = CAP * (1 - odd_pair)
    b = CAP * odd_pair
    first[0:CAP] = far[pl.ds(a, CAP)]
    first[CAP : 2 * CAP] = near[pl.ds(a, CAP)]
    second[0:CAP] = far[pl.ds(b, CAP)]
    second[CAP : 2 * CAP] = near[pl.ds(b, CAP)]


def faces(vel, d, wet, vel_next, d_next, wet_next):
    w = wet * wet_next
    speed = 0.5 * (vel + vel_next) * w
    mix = 0.5 * (d + d_next) * w
    return jnp.maximum(speed, 0.0) + mix, jnp.minimum(speed, 0.0) - mix


def stencil(wet, east, west, north, south):
    center = 1.0 - wet * (east[0] - west[1] + north[0] - south[1])
    return center, -wet * east[1], wet * west[0], -wet * north[1], wet * south[0]


def band_stencil(fields):
    d, u, v, wet = fields
    cols = d.shape[1]

    def moved(x, by, axis):
        if axis:
            return pltpu.roll(x, by % cols, 1)
        return jnp.concatenate([x[-by:], x[:-by]], axis=0)

    east = faces(u, d, wet, *(moved(x, -1, 1) for x in (u, d, wet)))
    north = faces(v, d, wet, *(moved(x, -1, 0) for x in (v, d, wet)))
    west = tuple(moved(x, 1, 1) for x in east)
    south = tuple(moved(x, 1, 0) for x in north)
    return stencil(wet, east, west, north, south)


def run_band(size, read, coef, base, buffers, pre, target):
    levels, _, cols = pre.shape
    src = read
    for step in range(1, STEPS + 1):
        new = []
        for n in range(step, size - step):
            c = src(n)
            k = [
                jnp.broadcast_to(coef[m, base + n : base + n + 1, :], (levels, cols))
                for m in range(5)
            ]
            value = (
                k[0] * c
                + k[1] * pltpu.roll(c, cols - 1, 1)
                + k[2] * pltpu.roll(c, 1, 1)
                + k[3] * src(n + 1)
                + k[4] * src(n - 1)
            )
            if step < STEPS:
                buffers[step % 2, n] = value
            else:
                new.append(value)
                if len(new) == SUB:
                    block = jnp.stack(new)
                    at = target + n - STEPS - SUB + 1
                    for l in range(0, levels, SUB):
                        pre[l : l + SUB, at : at + SUB, :] = jnp.swapaxes(
                            block[:, l : l + SUB], 0, 1
                        )
                    new = []
        src = lambda n, held=buffers.at[step % 2]: held[n]


def prepare_kernel(
    tracer_hbm, diff_hbm, zonal_hbm, merid_hbm, mask_hbm, weight_hbm, proj_hbm, recv_hbm,
    rows_out, across, top, bottom, fields, coef, weight, share, recv,
    tracer, mask, proj, sems,
):
    levels, rows, cols = tracer.shape
    sources = (tracer_hbm, diff_hbm, zonal_hbm, merid_hbm, mask_hbm, proj_hbm, weight_hbm, recv_hbm)
    targets = (tracer, fields.at[0], fields.at[1], fields.at[2], mask, proj, weight, recv)
    copies = [pltpu.make_async_copy(a, b, sems.at[k]) for k, (a, b) in enumerate(zip(sources, targets))]
    for copy in copies:
        copy.start()
    for copy in copies[1:6]:
        copy.wait()
    fields[3] = mask[...].astype(jnp.float32)
    for f in range(share.shape[0]):
        share[f] = jnp.broadcast_to(jnp.swapaxes(proj[f : f + 1, :], 0, 1), share.shape[1:])
    parts = [fields[f] for f in range(4)]
    zero = jnp.zeros((SUB, cols), jnp.float32)
    for y in range(0, rows, SUB):
        stacked = jnp.stack([x[y : y + SUB] for x in parts] + [zero] * (SUB - 4))
        across[y : y + SUB] = jnp.swapaxes(stacked, 0, 1)
    for f, x in enumerate(parts):
        bottom[f * STEPS : (f + 1) * STEPS, :] = x[0:STEPS]
        top[f * STEPS : (f + 1) * STEPS, :] = x[rows - STEPS : rows]
    for m, value in enumerate(band_stencil(parts)):
        coef[m] = value
    copies[0].wait()
    for y in range(0, rows, SUB):
        for l in range(0, levels, SUB):
            block = tracer[l : l + SUB, y : y + SUB, :]
            rows_out[y : y + SUB, l : l + SUB, :] = jnp.swapaxes(block, 0, 1)
    copies[6].wait()
    copies[7].wait()


def remap_kernel(
    bands, recv, own, near, first, second, weight, share, start, top, bottom,
    forced, contrib, here, there, tiles,
):
    rows, levels, cols = forced.shape
    width = weight.shape[1]
    across = cols // width
    odd_core, odd_pair = band_parity()
    tiles[2 * CAP : 3 * CAP] = own[...]

    def place(above, below):
        tiles[0:CAP] = above[0:CAP]
        tiles[4 * CAP : 5 * CAP] = below[0:CAP]

        @pl.when(odd_core == 0)
        def _():
            tiles[CAP : 2 * CAP] = near[0:CAP]
            tiles[3 * CAP : 4 * CAP] = below[CAP : 2 * CAP]

        @pl.when(odd_core == 1)
        def _():
            tiles[CAP : 2 * CAP] = above[CAP : 2 * CAP]
            tiles[3 * CAP : 4 * CAP] = near[CAP : 2 * CAP]

    @pl.when(odd_pair == 0)
    def _():
        place(first, second)

    @pl.when(odd_pair == 1)
    def _():
        place(second, first)

    band = lax.axis_index("lat")
    for s in range(weight.shape[0]):
        part = lax.dot_general(
            tiles[s], weight[s], (((1,), (1,)), ((), ())), preferred_element_type=jnp.float32
        )
        source = band + REACH - s // CAP
        part = jnp.where((source >= 0) & (source < bands), part, 0.0)
        contrib[s] = part
        update = share[0] * part[0:1, :]
        for f in range(1, share.shape[0]):
            update = update + share[f] * part[f : f + 1, :]
        t = recv[0, 0, s]
        y = jnp.minimum(lax.div(t, across), rows - 1)
        at = pl.ds(pl.multiple_of(lax.rem(t, across) * width, width), width)
        update = jnp.where(t < rows * across, update, 0.0)
        forced[y, :, at] = forced[y, :, at] + update

    @pl.when(odd_core == 0)
    def _():
        here[0:STEPS] = forced[rows - STEPS : rows]
        here[STEPS] = top[...]
        there[0:STEPS] = forced[0:STEPS]
        there[STEPS] = bottom[...]

    @pl.when(odd_core == 1)
    def _():
        here[0:STEPS] = forced[0:STEPS]
        here[STEPS] = bottom[...]
        there[0:STEPS] = forced[rows - STEPS : rows]
        there[STEPS] = top[...]


def flux_kernel(recv, contrib, flux, landed):
    fields, rows, cols = flux.shape
    width = contrib.shape[2]
    across = cols // width
    landed[...] = jnp.zeros_like(landed)
    for s in range(contrib.shape[0]):
        t = recv[0, 0, s]
        y = jnp.minimum(lax.div(t, across), rows - 1)
        k = lax.rem(t, across)
        part = jnp.where(t < rows * across, contrib[s], 0.0)
        landed[k, y] = landed[k, y] + part
    for k in range(across):
        for y in range(0, rows, SUB):
            block = jnp.swapaxes(landed[k, y : y + SUB], 0, 1)
            flux[:, y : y + SUB, k * width : (k + 1) * width] = block


def slot_masks(slots):
    wide = LANES // slots
    lane = lax.broadcasted_iota(jnp.int32, (1, LANES), 1)
    slot = lax.rem(lax.div(lane + wide // 2, wide), slots)
    place = lax.rem(lane + wide // 2, wide)
    return lane, slot, place, wide


def rolled(x, by):
    by = by % LANES
    return pltpu.roll(x, by, 1) if by else x


def slotted(row, i, wide, place):
    first = rolled(row[:, 0:LANES], wide * i + STEPS)
    last = rolled(row[:, row.shape[1] - LANES :], wide * i - STEPS)
    return jnp.where(place < wide // 2, last, first)


def inside_kernel(forced, across, coef, pre, packed, buffers):
    rows, levels, cols = forced.shape
    slots = rows // SUB
    _, slot, place, wide = slot_masks(slots)
    for part, base in ((forced, 0), (across, levels)):
        for l in range(0, part.shape[1], SUB):
            for q in range(SUB):
                tile = None
                for i in range(slots):
                    piece = slotted(part[SUB * i + q, l : l + SUB, :], i, wide, place)
                    tile = piece if tile is None else jnp.where(slot == i, piece, tile)
                packed[q, base + l : base + l + SUB, :] = tile
    size = rows - 2 * (SUB - STEPS)
    run_band(size, lambda n: forced[SUB - STEPS + n], coef, SUB - STEPS, buffers, pre, SUB)


def lane_reversed(x):
    tiles = []
    for k in range(x.shape[-1] // LANES - 1, -1, -1):
        block = x[:, k * LANES : (k + 1) * LANES]
        index = LANES - 1 - lax.broadcasted_iota(jnp.int32, block.shape, 1)
        tiles.append(jnp.take_along_axis(block, index, axis=1))
    return tiles


SIGNS = (1.0, -1.0, -1.0, 1.0)


def pack_kernel(top_band, here, there, packed, halo, static_halo, outer, edges):
    levels, cols = halo.shape[1:]
    odd_core, _ = band_parity()
    band = lax.axis_index("lat")
    fold = band == top_band - 1

    def straight(base, part):
        halo[base : base + STEPS] = part[0:STEPS]
        for f in range(4):
            static_halo[f, base : base + STEPS, :] = part[STEPS, f * STEPS : (f + 1) * STEPS, :]

    def folded(part):
        for i in range(STEPS):
            for l in range(0, levels, SUB):
                for n, block in enumerate(lane_reversed(part[STEPS - 1 - i, l : l + SUB, :])):
                    halo[i, l : l + SUB, n * LANES : (n + 1) * LANES] = block
        for r in range(0, 4 * STEPS, SUB):
            for n, block in enumerate(lane_reversed(part[STEPS, r : r + SUB, :])):
                for k in range(SUB):
                    f, i = divmod(r + k, STEPS)
                    static_halo[
                        f, STEPS - 1 - i : STEPS - i, n * LANES : (n + 1) * LANES
                    ] = SIGNS[f] * block[k : k + 1, :]

    @pl.when(odd_core == 0)
    def _():
        straight(0, here)

        @pl.when(band > 0)
        def _():
            straight(STEPS, there)

        @pl.when(band == 0)
        def _():
            halo[STEPS : 2 * STEPS] = jnp.zeros((STEPS, levels, cols), jnp.float32)
            for f in range(4):
                static_halo[f, STEPS : 2 * STEPS, :] = jnp.zeros((STEPS, cols), jnp.float32)

    @pl.when(odd_core == 1)
    def _():
        straight(STEPS, here)

        @pl.when(fold)
        def _():
            folded(there)

        @pl.when(jnp.logical_not(fold))
        def _():
            straight(0, there)

    slots = packed.shape[0] // 2
    lane, slot, place, wide = slot_masks(slots)
    zero = jnp.zeros((SUB, cols), jnp.float32)
    stacked = jnp.stack([static_halo[f] for f in range(4)] + [zero] * (SUB - 4))
    statics = jnp.swapaxes(stacked, 0, 1)
    for m in range(STEPS):
        for l in range(0, levels + SUB, SUB):
            if l < levels:
                above, below = halo[m, l : l + SUB, :], halo[STEPS + m, l : l + SUB, :]
            else:
                above, below = statics[m], statics[STEPS + m]
            north = slotted(above, slots - 1, wide, place)
            south = slotted(below, 0, wide, place)
            outer[m, l : l + SUB, :] = jnp.where(slot == 0, south, north)

    turn = lax.div(lax.rem(lane, wide), 2 * STEPS)
    is_first = lax.rem(lane, 2 * STEPS) < STEPS
    per = wide // (2 * STEPS)
    for g in range(3):
        total = None
        for m in range(per):
            tile = packed[g * per + m] if g < 2 else outer[m]
            first = rolled(tile, 2 * STEPS * m - STEPS)
            last = rolled(tile, 2 * STEPS * m + 3 * STEPS)
            piece = jnp.where(is_first, first, last)
            total = piece if total is None else jnp.where(turn == m, piece, total)
        edges[g] = total


def bands_kernel(forced, halo, fields, static_halo, held, pre, coef, buffers):
    rows, levels, cols = forced.shape
    size = SUB + 2 * STEPS
    low = [
        jnp.concatenate([static_halo[f, STEPS : 2 * STEPS], fields[f, 0 : size - STEPS]], axis=0)
        for f in range(4)
    ]
    high = [
        jnp.concatenate([fields[f, rows - size + STEPS : rows], static_halo[f, 0:STEPS]], axis=0)
        for f in range(4)
    ]
    for b, parts in enumerate((low, high)):
        for m, value in enumerate(band_stencil(parts)):
            coef[m, b * size : (b + 1) * size, :] = value
    del held

    def low_row(n):
        return halo[STEPS + n] if n < STEPS else forced[n - STEPS]

    def high_row(n):
        y = rows - size + STEPS + n
        return forced[y] if y < rows else halo[y - rows]

    run_band(size, low_row, coef, 0, buffers.at[0], pre, 0)
    run_band(size, high_row, coef, size, buffers.at[1], pre, rows - SUB)


def edge_kernel(pre, packed, outer, first, second, out, tiles, coef, stage, sems):
    levels, rows, cols = pre.shape
    slots = rows // SUB
    lane, slot, place, wide = slot_masks(slots)
    odd_block = lax.rem(lax.axis_index("lon"), 2)
    per = wide // (2 * STEPS)
    from_east = (lax.rem(lane, 2 * STEPS) < STEPS) == (odd_block == 0)
    outside = jnp.abs(2 * place - (wide - 1)) < 2 * STEPS
    depth = levels + SUB
    count = SUB + 2 * STEPS
    for l in range(0, depth, SUB):
        at = slice(l, l + SUB)
        got = [jnp.where(from_east, first[g, at], second[g, at]) for g in range(3)]
        inner = []
        for q in range(SUB):
            halo = rolled(got[q // per], -(2 * STEPS * (q % per) + STEPS))
            inner.append(jnp.where(outside, halo, packed[q, at]))
        for m in range(STEPS):
            halo = rolled(got[2], -(2 * STEPS * m + STEPS))
            beyond = jnp.where(outside, halo, outer[m, at])
            tiles[0, STEPS + SUB + m, at] = jnp.where(
                slot == slots - 1, beyond, rolled(inner[m], -wide)
            )
            tiles[0, m, at] = jnp.where(slot == 0, beyond, rolled(inner[SUB - STEPS + m], wide))
        for q in range(SUB):
            tiles[0, STEPS + q, at] = inner[q]

    def static(n, f):
        return jnp.broadcast_to(tiles[0, n, levels + f : levels + f + 1, :], (SUB, LANES))

    below = None
    now = [static(0, f) for f in range(4)]
    for n in range(count - 1):
        after = [static(n + 1, f) for f in range(4)]
        d, u, v, wet = now
        north = faces(v, d, wet, after[2], after[0], after[3])
        if n:
            east = faces(u, d, wet, rolled(u, -1), rolled(d, -1), rolled(wet, -1))
            west = tuple(rolled(x, 1) for x in east)
            for m, value in enumerate(stencil(wet, east, west, north, below)):
                coef[m, n] = value
        below, now = north, after
    for step in range(1, STEPS + 1):
        src, dst = (step - 1) % 2, step % 2
        for n in range(step, count - step):
            k = [coef[m, n] for m in range(5)]
            for l in range(0, levels, SUB):
                at = slice(l, l + SUB)
                c = tiles[src, n, at]
                tiles[dst, n, at] = (
                    k[0] * c
                    + k[1] * rolled(c, -1)
                    + k[2] * rolled(c, 1)
                    + k[3] * tiles[src, n + 1, at]
                    + k[4] * tiles[src, n - 1, at]
                )
    final = STEPS % 2
    copies = []
    for l in range(0, levels, SUB):
        block = jnp.stack([tiles[final, STEPS + q, l : l + SUB] for q in range(SUB)])
        turned = jnp.swapaxes(block, 0, 1)
        for k in range(SUB):
            for i in range(slots):
                y = slice(i * SUB, (i + 1) * SUB)
                low = rolled(turned[k], -(wide * i + STEPS))
                high = rolled(turned[k], -(wide * i - STEPS))
                body = pre[l + k, y, :]
                stage[l + k, y, 0:LANES] = jnp.where(lane < STEPS, low, body[:, 0:LANES])
                for x in range(LANES, cols - LANES, LANES):
                    stage[l + k, y, x : x + LANES] = body[:, x : x + LANES]
                stage[l + k, y, cols - LANES : cols] = jnp.where(
                    lane >= LANES - STEPS, high, body[:, cols - LANES : cols]
                )
        copy = pltpu.make_async_copy(
            stage.at[l : l + SUB], out.at[l : l + SUB], sems.at[l // SUB]
        )
        copy.start()
        copies.append(copy)
    for copy in copies:
        copy.wait()


def body(
    atm_flux,
    send_tile,
    recv_tile,
    remap_weight,
    tracer,
    diffusivity,
    zonal_velocity,
    merid_velocity,
    ocean_mask,
    level_proj,
):
    bands, blocks = lax.axis_size("lat"), lax.axis_size("lon")
    fields, width = atm_flux.shape[2:]
    levels, rows, cols = tracer.shape
    slots = remap_weight.shape[0]
    f32, bf16 = jnp.float32, jnp.bfloat16
    statics = (diffusivity, zonal_velocity, merid_velocity, ocean_mask)
    tile4 = ((2 * CAP, fields, width), bf16)

    core_pairs = swaps([(i, i + 1) for i in range(0, bands, 2)])
    chips = [(i, i + 1) for i in range(bands // 2 - 1)]
    even_chips = filled(swaps([(2 * a + k, 2 * b + k) for a, b in chips[0::2] for k in (0, 1)]), bands)
    odd_chips = filled(swaps([(2 * a + k, 2 * b + k) for a, b in chips[1::2] for k in (0, 1)]), bands)
    last = (bands - 1) * blocks
    across_chips = swaps(
        [(i * blocks + j, (i + 1) * blocks + j) for i in range(1, bands - 1, 2) for j in range(blocks)]
    ) + [(last + j, last + blocks - 1 - j) for j in range(blocks)]
    across_chips = filled(across_chips, bands * blocks)
    even_blocks = swaps([(j, j + 1) for j in range(0, blocks, 2)])
    odd_blocks = swaps([(j, (j + 1) % blocks) for j in range(1, blocks, 2)])

    near, far, own = call(
        gather_kernel,
        [tile4, tile4, ((CAP, fields, width), bf16)],
        [HB, HB],
        "gather",
        scratch=[
            pltpu.SMEM(send_tile.shape, jnp.int32),
            pltpu.VMEM(atm_flux.shape, bf16),
            pltpu.SemaphoreType.DMA((2,)),
        ],
    )(*in_hbm(send_tile, atm_flux))
    near_in = traded(near, "lat", core_pairs, "tile_core")
    first, second = call(relay_kernel, [tile4, tile4], [VM, VM], "relay")(far, near_in)
    first = traded(first, "lat", even_chips, "tile_even")
    second = traded(second, "lat", odd_chips, "tile_odd")
    start, across, top, bottom, parts, coef, weight, share, recv = call(
        prepare_kernel,
        [
            ((rows, levels, cols), f32),
            ((rows, SUB, cols), f32),
            ((4 * STEPS, cols), f32),
            ((4 * STEPS, cols), f32),
            ((4, rows, cols), f32),
            ((5, rows, cols), f32),
            (remap_weight.shape, bf16),
            ((fields, levels, width), f32),
            (recv_tile.shape, jnp.int32),
        ],
        [HB] * 8,
        "prepare",
        scratch=[
            pltpu.VMEM(tracer.shape, f32),
            pltpu.VMEM((rows, cols), jnp.int32),
            pltpu.VMEM((fields, levels), f32),
            pltpu.SemaphoreType.DMA((8,)),
        ],
    )(*in_hbm(tracer, *statics, remap_weight, level_proj.T, recv_tile))
    ring = ((STEPS + 1, levels, cols), f32)
    forced, contrib, here, there = call(
        functools.partial(remap_kernel, bands),
        [((rows, levels, cols), f32), ((slots, fields, width), f32), ring, ring],
        [SM] + [VM] * 9,
        "remap",
        scratch=[pltpu.VMEM((slots, fields, width), bf16)],
        aliases={7: 0},
    )(recv, own, near_in, first, second, weight, share, start, top, bottom)
    here = traded(here, "lat", core_pairs, "lat_core")
    there = traded(there, ("lat", "lon"), across_chips, "lat_chip")
    (ocean_flux,) = call(
        flux_kernel,
        [((fields, rows, cols), f32)],
        [SM, VM],
        "flux",
        scratch=[pltpu.VMEM((cols // width, rows, fields, width), f32)],
    )(recv, contrib)
    depth = levels + SUB
    count = SUB + 2 * STEPS
    pre, packed = call(
        inside_kernel,
        [((levels, rows, cols), f32), ((SUB, depth, LANES), f32)],
        [VM] * 3,
        "inside",
        scratch=[pltpu.VMEM((2, rows, levels, cols), f32)],
    )(forced, across, coef)
    halo, static_halo, outer, edges = call(
        functools.partial(pack_kernel, bands),
        [
            ((2 * STEPS, levels, cols), f32),
            ((4, 2 * STEPS, cols), f32),
            ((STEPS, depth, LANES), f32),
            ((3, depth, LANES), f32),
        ],
        [VM] * 3,
        "pack",
    )(here, there, packed)
    first = traded(edges, "lon", even_blocks, "lon_even")
    second = traded(edges, "lon", odd_blocks, "lon_odd")
    (pre,) = call(
        bands_kernel,
        [((levels, rows, cols), f32)],
        [VM] * 5,
        "bands",
        scratch=[
            pltpu.VMEM((5, 2 * count, cols), f32),
            pltpu.VMEM((2, 2, count, levels, cols), f32),
        ],
        aliases={4: 0},
    )(forced, halo, parts, static_halo, pre)
    (out,) = call(
        edge_kernel,
        [((levels, rows, cols), f32)],
        [VM] * 5,
        "edges",
        scratch=[
            pltpu.VMEM((2, count, depth, LANES), f32),
            pltpu.VMEM((5, count, SUB, LANES), f32),
            pltpu.VMEM((levels, rows, cols), f32),
            pltpu.SemaphoreType.DMA((levels // SUB,)),
        ],
        out_specs=[HB],
    )(pre, packed, outer, first, second)
    return (ocean_flux, out)


def solution(mesh):
    placed = (
        P("lat", None, None, "lon"),
        P("lat", "lon", None),
        P("lat", "lon", None),
        P("lat", None, "lon"),
        P(None, "lat", "lon"),
        P("lat", "lon"),
        P("lat", "lon"),
        P("lat", "lon"),
        P("lat", "lon"),
        P(),
    )
    return jax.shard_map(
        body,
        mesh=mesh,
        in_specs=placed,
        out_specs=(P(None, "lat", "lon"), P(None, "lat", "lon")),
        check_vma=False,
    )
```

```python
import functools

import jax
import jax.numpy as jnp
from jax import lax
from jax.experimental import pallas as pl
from jax.experimental.pallas import tpu as pltpu
from jax.sharding import PartitionSpec as P

CAP = 2
REACH = 2
STEPS = 4
LANES = 128
SUB = 8

VM = pl.BlockSpec(memory_space=pltpu.VMEM)
SM = pl.BlockSpec(memory_space=pltpu.SMEM)
HB = pl.BlockSpec(memory_space=pltpu.HBM)


def call(kernel, outs, in_specs, name, scratch=(), aliases=None, limit=12, out_specs=None):
    run = pl.pallas_call(
        kernel,
        out_shape=[jax.ShapeDtypeStruct(s, d) for s, d in outs],
        in_specs=in_specs,
        out_specs=out_specs or [VM] * len(outs),
        scratch_shapes=list(scratch),
        input_output_aliases=aliases or {},
        compiler_params=pltpu.CompilerParams(vmem_limit_bytes=limit << 20),
        name=name,
    )

    def scoped(*args):
        with jax.named_scope("run_" + name):
            return run(*args)

    return scoped


def in_hbm(*arrays):
    return [pltpu.with_memory_space_constraint(x, pltpu.HBM) for x in arrays]


def filled(routes, size):
    busy = {a for a, _ in routes}
    free = [i for i in range(size) if i not in busy]
    return routes + swaps(list(zip(free[0::2], free[1::2])))


def traded(x, axis, pairs, name):
    with jax.named_scope(name):
        return lax.ppermute(x, axis, pairs)


def swaps(pairs):
    return [route for a, b in pairs for route in ((a, b), (b, a))]


def region(step):
    pl.when(lax.axis_index("lat") >= 0)(step)


def band_parity():
    band = lax.axis_index("lat")
    return lax.rem(band, 2), lax.rem(lax.div(band, 2), 2)


def gather_kernel(send_hbm, atm_hbm, core, side, even, odd, own, send, atm, sems):
    copies = [
        pltpu.make_async_copy(send_hbm, send, sems.at[0]),
        pltpu.make_async_copy(atm_hbm, atm, sems.at[1]),
    ]
    for copy in copies:
        copy.start()
    for copy in copies:
        copy.wait()
    odd_core, odd_pair = band_parity()
    goes = (
        (core, 3 - 2 * odd_core),
        (side, 1 + 2 * odd_core),
        (even, 4 - 4 * odd_pair),
        (odd, 4 * odd_pair),
        (own, 2),
    )
    for target, d in goes:
        for c in range(CAP):
            target[c] = atm[0, send[0, 0, d * CAP + c]]


def faces(vel, d, wet, vel_next, d_next, wet_next):
    w = wet * wet_next
    speed = 0.5 * (vel + vel_next) * w
    mix = 0.5 * (d + d_next) * w
    return jnp.maximum(speed, 0.0) + mix, jnp.minimum(speed, 0.0) - mix


def stencil(wet, east, west, north, south):
    center = 1.0 - wet * (east[0] - west[1] + north[0] - south[1])
    return center, -wet * east[1], wet * west[0], -wet * north[1], wet * south[0]


def band_stencil(fields):
    d, u, v, wet = fields
    cols = d.shape[1]

    def moved(x, by, axis):
        if axis:
            return pltpu.roll(x, by % cols, 1)
        return jnp.concatenate([x[-by:], x[:-by]], axis=0)

    east = faces(u, d, wet, *(moved(x, -1, 1) for x in (u, d, wet)))
    north = faces(v, d, wet, *(moved(x, -1, 0) for x in (v, d, wet)))
    west = tuple(moved(x, 1, 1) for x in east)
    south = tuple(moved(x, 1, 0) for x in north)
    return stencil(wet, east, west, north, south)


def run_band(size, read, coef, base, buffers, pre, target):
    levels, _, cols = pre.shape
    src = read
    for step in range(1, STEPS + 1):
        new = []
        for n in range(step, size - step):
            c = src(n)
            k = [
                jnp.broadcast_to(coef[m, base + n : base + n + 1, :], (levels, cols))
                for m in range(5)
            ]
            value = (
                k[0] * c
                + k[1] * pltpu.roll(c, cols - 1, 1)
                + k[2] * pltpu.roll(c, 1, 1)
                + k[3] * src(n + 1)
                + k[4] * src(n - 1)
            )
            if step < STEPS:
                buffers[step % 2, n] = value
            else:
                new.append(value)
                if len(new) == SUB:
                    block = jnp.stack(new)
                    at = target + n - STEPS - SUB + 1
                    for l in range(0, levels, SUB):
                        pre[l : l + SUB, at : at + SUB, :] = jnp.swapaxes(
                            block[:, l : l + SUB], 0, 1
                        )
                    new = []
        src = lambda n, held=buffers.at[step % 2]: held[n]


def prepare_kernel(
    tracer_hbm, diff_hbm, zonal_hbm, merid_hbm, mask_hbm, weight_hbm, proj_hbm, recv_hbm,
    rows_out, across, top, bottom, fields, coef, weight, share, recv,
    tracer, mask, proj, sems,
):
    levels, rows, cols = tracer.shape
    sources = (tracer_hbm, diff_hbm, zonal_hbm, merid_hbm, mask_hbm, proj_hbm, weight_hbm, recv_hbm)
    targets = (tracer, fields.at[0], fields.at[1], fields.at[2], mask, proj, weight, recv)
    copies = [pltpu.make_async_copy(a, b, sems.at[k]) for k, (a, b) in enumerate(zip(sources, targets))]
    for copy in copies:
        copy.start()
    for copy in copies[1:6]:
        copy.wait()
    fields[3] = mask[...].astype(jnp.float32)
    for f in range(share.shape[0]):
        share[f] = jnp.broadcast_to(jnp.swapaxes(proj[f : f + 1, :], 0, 1), share.shape[1:])
    parts = [fields[f] for f in range(4)]
    zero = jnp.zeros((SUB, cols), jnp.float32)
    for y in range(0, rows, SUB):
        stacked = jnp.stack([x[y : y + SUB] for x in parts] + [zero] * (SUB - 4))
        across[y : y + SUB] = jnp.swapaxes(stacked, 0, 1)
    for f, x in enumerate(parts):
        bottom[f * STEPS : (f + 1) * STEPS, :] = x[0:STEPS]
        top[f * STEPS : (f + 1) * STEPS, :] = x[rows - STEPS : rows]
    for m, value in enumerate(band_stencil(parts)):
        coef[m] = value
    copies[0].wait()
    for y in range(0, rows, SUB):
        for l in range(0, levels, SUB):
            block = tracer[l : l + SUB, y : y + SUB, :]
            rows_out[y : y + SUB, l : l + SUB, :] = jnp.swapaxes(block, 0, 1)
    copies[6].wait()
    copies[7].wait()


def remap_kernel(
    bands, recv, own, core, side, even, odd, weight, share, start, top, bottom,
    forced, contrib, here, there, tiles,
):
    goal = recv[0].astype(jnp.float32)
    index = lax.broadcasted_iota(jnp.int32, goal.shape, 1)
    goals = [jnp.sum(jnp.where(index == s, goal, 0.0)).astype(jnp.int32) for s in range(goal.shape[1])]
    rows, levels, cols = forced.shape
    width = weight.shape[1]
    across = cols // width
    odd_core, odd_pair = band_parity()
    tiles[2 * CAP : 3 * CAP] = own[...]

    def place(d, part):
        tiles[d * CAP : (d + 1) * CAP] = part[...]

    @pl.when(odd_pair == 0)
    def _():
        place(0, even)
        place(4, odd)

    @pl.when(odd_pair == 1)
    def _():
        place(0, odd)
        place(4, even)

    @pl.when(odd_core == 0)
    def _():
        place(1, core)
        place(3, side)

    @pl.when(odd_core == 1)
    def _():
        place(1, side)
        place(3, core)

    band = lax.axis_index("lat")
    updates = []
    for s in range(weight.shape[0]):
        part = lax.dot_general(
            tiles[s], weight[s], (((1,), (1,)), ((), ())), preferred_element_type=jnp.float32
        )
        source = band + REACH - s // CAP
        part = jnp.where((source >= 0) & (source < bands), part, 0.0)
        contrib[s] = part
        update = share[0] * part[0:1, :]
        for f in range(1, share.shape[0]):
            update = update + share[f] * part[f : f + 1, :]
        updates.append(update)
    for t, update in zip(goals, updates):
        y = jnp.minimum(lax.div(t, across), rows - 1)
        at = pl.ds(pl.multiple_of(lax.rem(t, across) * width, width), width)
        update = jnp.where(t < rows * across, update, 0.0)
        forced[y, :, at] = forced[y, :, at] + update

    @pl.when(odd_core == 0)
    def _():
        here[0:STEPS] = forced[rows - STEPS : rows]
        here[STEPS] = top[...]
        there[0:STEPS] = forced[0:STEPS]
        there[STEPS] = bottom[...]

    @pl.when(odd_core == 1)
    def _():
        here[0:STEPS] = forced[0:STEPS]
        here[STEPS] = bottom[...]
        there[0:STEPS] = forced[rows - STEPS : rows]
        there[STEPS] = top[...]


def land_flux(recv, contrib, flux, landed):
    fields, rows, cols = flux.shape
    width = contrib.shape[2]
    across = cols // width
    landed[...] = jnp.zeros_like(landed)
    for s in range(contrib.shape[0]):
        t = recv[0, 0, s]
        y = jnp.minimum(lax.div(t, across), rows - 1)
        k = lax.rem(t, across)
        part = jnp.where(t < rows * across, contrib[s], 0.0)
        landed[k, y] = landed[k, y] + part
    for k in range(across):
        for y in range(0, rows, SUB):
            block = jnp.swapaxes(landed[k, y : y + SUB], 0, 1)
            flux[:, y : y + SUB, k * width : (k + 1) * width] = block


def slot_masks(slots):
    wide = LANES // slots
    lane = lax.broadcasted_iota(jnp.int32, (1, LANES), 1)
    slot = lax.rem(lax.div(lane + wide // 2, wide), slots)
    place = lax.rem(lane + wide // 2, wide)
    return lane, slot, place, wide


def rolled(x, by):
    by = by % LANES
    return pltpu.roll(x, by, 1) if by else x


def slotted(row, i, wide, place):
    first = rolled(row[:, 0:LANES], wide * i + STEPS)
    last = rolled(row[:, row.shape[1] - LANES :], wide * i - STEPS)
    return jnp.where(place < wide // 2, last, first)


def inside_kernel(forced, across, coef, pre, packed, buffers):
    rows, levels, cols = forced.shape
    slots = rows // SUB
    _, slot, place, wide = slot_masks(slots)
    for part, base in ((forced, 0), (across, levels)):
        for l in range(0, part.shape[1], SUB):
            for q in range(SUB):
                tile = None
                for i in range(slots):
                    piece = slotted(part[SUB * i + q, l : l + SUB, :], i, wide, place)
                    tile = piece if tile is None else jnp.where(slot == i, piece, tile)
                packed[q, base + l : base + l + SUB, :] = tile
    size = rows - 2 * (SUB - STEPS)
    run_band(size, lambda n: forced[SUB - STEPS + n], coef, SUB - STEPS, buffers, pre, SUB)


def lane_reversed(x):
    tiles = []
    for k in range(x.shape[-1] // LANES - 1, -1, -1):
        block = x[:, k * LANES : (k + 1) * LANES]
        index = LANES - 1 - lax.broadcasted_iota(jnp.int32, block.shape, 1)
        tiles.append(jnp.take_along_axis(block, index, axis=1))
    return tiles


SIGNS = (1.0, -1.0, -1.0, 1.0)


def pack_kernel(top_band, here, there, packed, halo, static_halo, outer, even, odd):
    levels, cols = halo.shape[1:]
    odd_core, _ = band_parity()
    band = lax.axis_index("lat")
    fold = band == top_band - 1

    def straight(base, part):
        halo[base : base + STEPS] = part[0:STEPS]
        for f in range(4):
            static_halo[f, base : base + STEPS, :] = part[STEPS, f * STEPS : (f + 1) * STEPS, :]

    def folded(part):
        for i in range(STEPS):
            for l in range(0, levels, SUB):
                for n, block in enumerate(lane_reversed(part[STEPS - 1 - i, l : l + SUB, :])):
                    halo[i, l : l + SUB, n * LANES : (n + 1) * LANES] = block
        for r in range(0, 4 * STEPS, SUB):
            for n, block in enumerate(lane_reversed(part[STEPS, r : r + SUB, :])):
                for k in range(SUB):
                    f, i = divmod(r + k, STEPS)
                    static_halo[
                        f, STEPS - 1 - i : STEPS - i, n * LANES : (n + 1) * LANES
                    ] = SIGNS[f] * block[k : k + 1, :]

    @pl.when(odd_core == 0)
    def _():
        straight(0, here)

        @pl.when(band > 0)
        def _():
            straight(STEPS, there)

        @pl.when(band == 0)
        def _():
            halo[STEPS : 2 * STEPS] = jnp.zeros((STEPS, levels, cols), jnp.float32)
            for f in range(4):
                static_halo[f, STEPS : 2 * STEPS, :] = jnp.zeros((STEPS, cols), jnp.float32)

    @pl.when(odd_core == 1)
    def _():
        straight(STEPS, here)

        @pl.when(fold)
        def _():
            folded(there)

        @pl.when(jnp.logical_not(fold))
        def _():
            straight(0, there)

    slots = packed.shape[0] // 2
    lane, slot, place, wide = slot_masks(slots)
    zero = jnp.zeros((SUB, cols), jnp.float32)
    stacked = jnp.stack([static_halo[f] for f in range(4)] + [zero] * (SUB - 4))
    statics = jnp.swapaxes(stacked, 0, 1)
    for m in range(STEPS):
        for l in range(0, levels + SUB, SUB):
            if l < levels:
                above, below = halo[m, l : l + SUB, :], halo[STEPS + m, l : l + SUB, :]
            else:
                above, below = statics[m], statics[STEPS + m]
            north = slotted(above, slots - 1, wide, place)
            south = slotted(below, 0, wide, place)
            outer[m, l : l + SUB, :] = jnp.where(slot == 0, south, north)

    depth = packed.shape[1]
    lane = jnp.broadcast_to(lane, (SUB, LANES))
    turn = lax.div(lax.rem(lane, wide), STEPS)
    spot = lax.div(lane, STEPS)
    odd_block = lax.rem(lax.axis_index("lon"), 2)

    def columns(begin, targets):
        for a in range(depth // SUB):
            at = slice(a * SUB, (a + 1) * SUB)
            total = rolled(packed[0, at], -begin)
            for q in range(1, SUB):
                total = jnp.where(turn == q, rolled(packed[q, at], STEPS * q - begin), total)
            targets[at, :] = total
        total = None
        for a in range(depth // SUB):
            for m in range(STEPS):
                tile = outer[m, a * SUB : (a + 1) * SUB]
                k = a * (wide // STEPS) + m
                for slot_of, where in ((slots - 1, k), (0, k + STEPS)):
                    piece = rolled(tile, STEPS * where - begin - wide * slot_of)
                    total = piece if total is None else jnp.where(spot == where, piece, total)
        targets[depth : depth + SUB, :] = total

    first, last = STEPS, -2 * STEPS

    @pl.when(odd_block == 0)
    def _():
        columns(last, even)
        columns(first, odd)

    @pl.when(odd_block == 1)
    def _():
        columns(first, even)
        columns(last, odd)


def bands_kernel(
    recv, contrib, forced, halo, fields, static_halo, held, pre, flux_hbm,
    coef, buffers, landed, flux, sem,
):
    rows, levels, cols = forced.shape
    del held
    land_flux(recv, contrib, flux, landed)
    copy = pltpu.make_async_copy(flux, flux_hbm, sem)
    copy.start()

    @region
    def _():
        size = SUB + 2 * STEPS
        low = [
            jnp.concatenate([static_halo[f, STEPS : 2 * STEPS], fields[f, 0 : size - STEPS]], axis=0)
            for f in range(4)
        ]
        high = [
            jnp.concatenate([fields[f, rows - size + STEPS : rows], static_halo[f, 0:STEPS]], axis=0)
            for f in range(4)
        ]
        for b, parts in enumerate((low, high)):
            for m, value in enumerate(band_stencil(parts)):
                coef[m, b * size : (b + 1) * size, :] = value

        def low_row(n):
            return halo[STEPS + n] if n < STEPS else forced[n - STEPS]

        def high_row(n):
            y = rows - size + STEPS + n
            return forced[y] if y < rows else halo[y - rows]

        run_band(size, low_row, coef, 0, buffers.at[0], pre, 0)
        run_band(size, high_row, coef, size, buffers.at[1], pre, rows - SUB)

    copy.wait()


def edge_kernel(pre, packed, outer, even, odd, out, tiles, fixed, coef, stage, sems):
    levels, rows, cols = pre.shape
    slots = rows // SUB
    lane, slot, place, wide = slot_masks(slots)
    odd_block = lax.rem(lax.axis_index("lon"), 2)
    depth = levels + SUB
    count = SUB + 2 * STEPS
    lane = jnp.broadcast_to(lane, (SUB, LANES))
    east_even = jnp.broadcast_to(odd_block == 0, (SUB, LANES))
    from_east = lax.div(place, STEPS) == wide // 2 // STEPS - 1
    from_west = lax.div(place, STEPS) == wide // 2 // STEPS

    def ends(at):
        return (
            jnp.where(east_even, even[at], odd[at]),
            jnp.where(east_even, odd[at], even[at]),
        )

    def joined(pair, tile, shift):
        tile = jnp.where(from_east, rolled(pair[0], shift - STEPS), tile)
        return jnp.where(from_west, rolled(pair[1], shift), tile)

    far = ends(slice(depth, depth + SUB))
    for a in range(depth // SUB):
        at = slice(a * SUB, (a + 1) * SUB)
        pair = ends(at)
        inner = [joined(pair, packed[q, at], -STEPS * q) for q in range(SUB)]
        placed = [None] * count
        for m in range(STEPS):
            k = STEPS * (a * (wide // STEPS) + m)
            north = joined(far, outer[m, at], wide * (slots - 1) - k)
            south = joined(far, outer[m, at], -k - STEPS * STEPS)
            placed[STEPS + SUB + m] = jnp.where(slot == slots - 1, north, rolled(inner[m], -wide))
            placed[m] = jnp.where(slot == 0, south, rolled(inner[SUB - STEPS + m], wide))
        placed[STEPS : STEPS + SUB] = inner
        for n in range(count):
            if a * SUB < levels:
                tiles[0, n, at] = placed[n]
            else:
                fixed[n * SUB : (n + 1) * SUB, :] = placed[n]

    fields = [fixed[pl.ds(f, count, stride=SUB), :] for f in range(4)]
    for m, value in enumerate(band_stencil(fields)):
        coef[m] = value
    for step in range(1, STEPS + 1):
        src, dst = (step - 1) % 2, step % 2
        for n in range(step, count - step):
            k = [jnp.broadcast_to(coef[m, n : n + 1, :], (SUB, LANES)) for m in range(5)]
            for l in range(0, levels, SUB):
                at = slice(l, l + SUB)
                c = tiles[src, n, at]
                tiles[dst, n, at] = (
                    k[0] * c
                    + k[1] * rolled(c, -1)
                    + k[2] * rolled(c, 1)
                    + k[3] * tiles[src, n + 1, at]
                    + k[4] * tiles[src, n - 1, at]
                )
    final = STEPS % 2
    copies = []
    group = 4
    for l in range(0, levels, group):
        part = slice(l, l + group)
        copy = pltpu.make_async_copy(stage.at[part], out.at[part], sems.at[l // group])
        copies.append(copy)

        @region
        def _(l=l, copy=copy):
            at = slice(l // SUB * SUB, l // SUB * SUB + SUB)
            block = jnp.stack([tiles[final, STEPS + q, at] for q in range(SUB)])
            turned = jnp.swapaxes(block, 0, 1)
            for k in range(l, l + group):
                tile = turned[k % SUB]
                for i in range(slots):
                    y = slice(i * SUB, (i + 1) * SUB)
                    low = rolled(tile, -(wide * i + STEPS))
                    high = rolled(tile, -(wide * i - STEPS))
                    body = pre[k, y, :]
                    stage[k, y, 0:LANES] = jnp.where(lane < STEPS, low, body[:, 0:LANES])
                    for x in range(LANES, cols - LANES, LANES):
                        stage[k, y, x : x + LANES] = body[:, x : x + LANES]
                    stage[k, y, cols - LANES : cols] = jnp.where(
                        lane >= LANES - STEPS, high, body[:, cols - LANES : cols]
                    )
            copy.start()

    for copy in copies:
        copy.wait()


def body(
    atm_flux,
    send_tile,
    recv_tile,
    remap_weight,
    tracer,
    diffusivity,
    zonal_velocity,
    merid_velocity,
    ocean_mask,
    level_proj,
):
    bands, blocks = lax.axis_size("lat"), lax.axis_size("lon")
    fields, width = atm_flux.shape[2:]
    levels, rows, cols = tracer.shape
    slots = remap_weight.shape[0]
    f32, bf16 = jnp.float32, jnp.bfloat16
    statics = (diffusivity, zonal_velocity, merid_velocity, ocean_mask)

    core_pairs = swaps([(i, i + 1) for i in range(0, bands, 2)])
    chips = [(i, i + 1) for i in range(bands // 2 - 1)]
    even_chips = filled(swaps([(2 * a + k, 2 * b + k) for a, b in chips[0::2] for k in (0, 1)]), bands)
    odd_chips = filled(swaps([(2 * a + k, 2 * b + k) for a, b in chips[1::2] for k in (0, 1)]), bands)
    last = (bands - 1) * blocks
    beside = swaps(
        [(i * blocks + j, (i + 1) * blocks + j) for i in range(1, bands - 1, 2) for j in range(blocks)]
    )
    fold = [(last + j, last + blocks - 1 - j) for j in range(blocks)]
    across_chips = filled(beside + fold, bands * blocks)
    beside = filled(beside, bands * blocks)
    even_blocks = swaps([(j, j + 1) for j in range(0, blocks, 2)])
    odd_blocks = swaps([(j, (j + 1) % blocks) for j in range(1, blocks, 2)])

    tile2 = ((CAP, fields, width), bf16)
    core, side, even, odd, own = call(
        gather_kernel,
        [tile2] * 5,
        [HB, HB],
        "gather",
        scratch=[
            pltpu.SMEM(send_tile.shape, jnp.int32),
            pltpu.VMEM(atm_flux.shape, bf16),
            pltpu.SemaphoreType.DMA((2,)),
        ],
    )(*in_hbm(send_tile, atm_flux))
    core = traded(core, "lat", core_pairs, "tile_core")
    even = traded(even, "lat", even_chips, "tile_even")
    odd = traded(odd, "lat", odd_chips, "tile_odd")
    side = traded(side, ("lat", "lon"), beside, "tile_side")
    start, across, top, bottom, parts, coef, weight, share, recv = call(
        prepare_kernel,
        [
            ((rows, levels, cols), f32),
            ((rows, SUB, cols), f32),
            ((4 * STEPS, cols), f32),
            ((4 * STEPS, cols), f32),
            ((4, rows, cols), f32),
            ((5, rows, cols), f32),
            (remap_weight.shape, bf16),
            ((fields, levels, width), f32),
            (recv_tile.shape, jnp.int32),
        ],
        [HB] * 8,
        "prepare",
        scratch=[
            pltpu.VMEM(tracer.shape, f32),
            pltpu.VMEM((rows, cols), jnp.int32),
            pltpu.VMEM((fields, levels), f32),
            pltpu.SemaphoreType.DMA((8,)),
        ],
    )(*in_hbm(tracer, *statics, remap_weight, level_proj.T, recv_tile))
    ring = ((STEPS + 1, levels, cols), f32)
    forced, contrib, here, there = call(
        functools.partial(remap_kernel, bands),
        [((rows, levels, cols), f32), ((slots, fields, width), f32), ring, ring],
        [VM] * 11,
        "remap",
        scratch=[
            pltpu.VMEM((slots, fields, width), bf16),
        ],
        aliases={8: 0},
    )(recv, own, core, side, even, odd, weight, share, start, top, bottom)
    here = traded(here, "lat", core_pairs, "lat_core")
    there = traded(there, ("lat", "lon"), across_chips, "lat_chip")
    depth = levels + SUB
    count = SUB + 2 * STEPS
    pre, packed = call(
        inside_kernel,
        [((levels, rows, cols), f32), ((SUB, depth, LANES), f32)],
        [VM] * 3,
        "inside",
        scratch=[pltpu.VMEM((2, rows, levels, cols), f32)],
    )(forced, across, coef)
    halo, static_halo, outer, even, odd = call(
        functools.partial(pack_kernel, bands),
        [
            ((2 * STEPS, levels, cols), f32),
            ((4, 2 * STEPS, cols), f32),
            ((STEPS, depth, LANES), f32),
            ((depth + SUB, LANES), f32),
            ((depth + SUB, LANES), f32),
        ],
        [VM] * 3,
        "pack",
    )(here, there, packed)
    even = traded(even, "lon", even_blocks, "lon_even")
    odd = traded(odd, "lon", odd_blocks, "lon_odd")
    pre, ocean_flux = call(
        bands_kernel,
        [((levels, rows, cols), f32), ((fields, rows, cols), f32)],
        [SM] + [VM] * 6,
        "bands",
        scratch=[
            pltpu.VMEM((5, 2 * count, cols), f32),
            pltpu.VMEM((2, 2, count, levels, cols), f32),
            pltpu.VMEM((cols // width, rows, fields, width), f32),
            pltpu.VMEM((fields, rows, cols), f32),
            pltpu.SemaphoreType.DMA(()),
        ],
        aliases={6: 0},
        out_specs=[VM, HB],
    )(recv, contrib, forced, halo, parts, static_halo, pre)
    (out,) = call(
        edge_kernel,
        [((levels, rows, cols), f32)],
        [VM] * 5,
        "edges",
        scratch=[
            pltpu.VMEM((2, count, levels, LANES), f32),
            pltpu.VMEM((count * SUB, LANES), f32),
            pltpu.VMEM((5, count, LANES), f32),
            pltpu.VMEM((levels, rows, cols), f32),
            pltpu.SemaphoreType.DMA((levels // 4,)),
        ],
        out_specs=[HB],
    )(pre, packed, outer, even, odd)
    return (ocean_flux, out)


def solution(mesh):
    placed = (
        P("lat", None, None, "lon"),
        P("lat", "lon", None),
        P("lat", "lon", None),
        P("lat", None, "lon"),
        P(None, "lat", "lon"),
        P("lat", "lon"),
        P("lat", "lon"),
        P("lat", "lon"),
        P("lat", "lon"),
        P(),
    )
    return jax.shard_map(
        body,
        mesh=mesh,
        in_specs=placed,
        out_specs=(P(None, "lat", "lon"), P(None, "lat", "lon")),
        check_vma=False,
    )
```

```python
import functools

import jax
import jax.numpy as jnp
from jax import lax
from jax.experimental import pallas as pl
from jax.experimental.pallas import tpu as pltpu
from jax.sharding import PartitionSpec as P

CAP = 2
REACH = 2
STEPS = 4
LANES = 128
SUB = 8

VM = pl.BlockSpec(memory_space=pltpu.VMEM)
SM = pl.BlockSpec(memory_space=pltpu.SMEM)
HB = pl.BlockSpec(memory_space=pltpu.HBM)


def call(kernel, outs, in_specs, name, scratch=(), aliases=None, limit=12, out_specs=None):
    run = pl.pallas_call(
        kernel,
        out_shape=[jax.ShapeDtypeStruct(s, d) for s, d in outs],
        in_specs=in_specs,
        out_specs=out_specs or [VM] * len(outs),
        scratch_shapes=list(scratch),
        input_output_aliases=aliases or {},
        compiler_params=pltpu.CompilerParams(vmem_limit_bytes=limit << 20),
        name=name,
    )

    def scoped(*args):
        with jax.named_scope("run_" + name):
            return run(*args)

    return scoped


def in_hbm(*arrays):
    return [pltpu.with_memory_space_constraint(x, pltpu.HBM) for x in arrays]


def filled(routes, size):
    busy = {a for a, _ in routes}
    free = [i for i in range(size) if i not in busy]
    return routes + swaps(list(zip(free[0::2], free[1::2])))


def traded(x, axis, pairs, name):
    with jax.named_scope(name):
        return lax.ppermute(x, axis, pairs)


def swaps(pairs):
    return [route for a, b in pairs for route in ((a, b), (b, a))]


def region(step):
    pl.when(lax.axis_index("lat") >= 0)(step)


def band_parity():
    band = lax.axis_index("lat")
    return lax.rem(band, 2), lax.rem(lax.div(band, 2), 2)


def gather_kernel(send_hbm, atm_hbm, core, side, even, odd, own, send, atm, sems):
    copies = [
        pltpu.make_async_copy(send_hbm, send, sems.at[0]),
        pltpu.make_async_copy(atm_hbm, atm, sems.at[1]),
    ]
    for copy in copies:
        copy.start()
    for copy in copies:
        copy.wait()
    odd_core, odd_pair = band_parity()
    goes = (
        (core, 3 - 2 * odd_core),
        (side, 1 + 2 * odd_core),
        (even, 4 - 4 * odd_pair),
        (odd, 4 * odd_pair),
        (own, 2),
    )
    for target, d in goes:
        for c in range(CAP):
            target[c] = atm[0, send[0, 0, d * CAP + c]]


def faces(vel, d, wet, vel_next, d_next, wet_next):
    w = wet * wet_next
    speed = 0.5 * (vel + vel_next) * w
    mix = 0.5 * (d + d_next) * w
    return jnp.maximum(speed, 0.0) + mix, jnp.minimum(speed, 0.0) - mix


def stencil(wet, east, west, north, south):
    center = 1.0 - wet * (east[0] - west[1] + north[0] - south[1])
    return center, -wet * east[1], wet * west[0], -wet * north[1], wet * south[0]


def band_stencil(fields):
    d, u, v, wet = fields
    cols = d.shape[1]

    def moved(x, by, axis):
        if axis:
            return pltpu.roll(x, by % cols, 1)
        return jnp.concatenate([x[-by:], x[:-by]], axis=0)

    east = faces(u, d, wet, *(moved(x, -1, 1) for x in (u, d, wet)))
    north = faces(v, d, wet, *(moved(x, -1, 0) for x in (v, d, wet)))
    west = tuple(moved(x, 1, 1) for x in east)
    south = tuple(moved(x, 1, 0) for x in north)
    return stencil(wet, east, west, north, south)


def run_band(size, read, coef, base, buffers, pre, target):
    levels, _, cols = pre.shape
    src = read
    for step in range(1, STEPS + 1):
        new = []
        for n in range(step, size - step):
            c = src(n)
            k = [
                jnp.broadcast_to(coef[m, base + n : base + n + 1, :], (levels, cols))
                for m in range(5)
            ]
            value = (
                k[0] * c
                + k[1] * pltpu.roll(c, cols - 1, 1)
                + k[2] * pltpu.roll(c, 1, 1)
                + k[3] * src(n + 1)
                + k[4] * src(n - 1)
            )
            if step < STEPS:
                buffers[step % 2, n] = value
            else:
                new.append(value)
                if len(new) == SUB:
                    block = jnp.stack(new)
                    at = target + n - STEPS - SUB + 1
                    for l in range(0, levels, SUB):
                        pre[l : l + SUB, at : at + SUB, :] = jnp.swapaxes(
                            block[:, l : l + SUB], 0, 1
                        )
                    new = []
        src = lambda n, held=buffers.at[step % 2]: held[n]


def prepare_kernel(
    tracer_hbm, diff_hbm, zonal_hbm, merid_hbm, mask_hbm, weight_hbm, proj_hbm, recv_hbm,
    rows_out, across, top, bottom, fields, coef, weight, share, recv,
    tracer, mask, proj, sems,
):
    levels, rows, cols = tracer.shape
    sources = (tracer_hbm, diff_hbm, zonal_hbm, merid_hbm, mask_hbm, proj_hbm, weight_hbm, recv_hbm)
    targets = (tracer, fields.at[0], fields.at[1], fields.at[2], mask, proj, weight, recv)
    copies = [pltpu.make_async_copy(a, b, sems.at[k]) for k, (a, b) in enumerate(zip(sources, targets))]
    for copy in copies:
        copy.start()
    for copy in copies[1:6]:
        copy.wait()
    fields[3] = mask[...].astype(jnp.float32)
    for f in range(share.shape[0]):
        share[f] = jnp.broadcast_to(jnp.swapaxes(proj[f : f + 1, :], 0, 1), share.shape[1:])
    parts = [fields[f] for f in range(4)]
    zero = jnp.zeros((SUB, cols), jnp.float32)
    for y in range(0, rows, SUB):
        stacked = jnp.stack([x[y : y + SUB] for x in parts] + [zero] * (SUB - 4))
        across[y : y + SUB] = jnp.swapaxes(stacked, 0, 1)
    for f, x in enumerate(parts):
        bottom[f * STEPS : (f + 1) * STEPS, :] = x[0:STEPS]
        top[f * STEPS : (f + 1) * STEPS, :] = x[rows - STEPS : rows]
    for m, value in enumerate(band_stencil(parts)):
        coef[m] = value
    copies[0].wait()
    for y in range(0, rows, SUB):
        for l in range(0, levels, SUB):
            block = tracer[l : l + SUB, y : y + SUB, :]
            rows_out[y : y + SUB, l : l + SUB, :] = jnp.swapaxes(block, 0, 1)
    copies[6].wait()
    copies[7].wait()


def remap_kernel(
    bands, recv, own, core, side, even, odd, weight, share, start, top, bottom,
    forced, contrib, here, there, tiles,
):
    goal = recv[0].astype(jnp.float32)
    index = lax.broadcasted_iota(jnp.int32, goal.shape, 1)
    goals = [jnp.sum(jnp.where(index == s, goal, 0.0)).astype(jnp.int32) for s in range(goal.shape[1])]
    rows, levels, cols = forced.shape
    width = weight.shape[1]
    across = cols // width
    odd_core, odd_pair = band_parity()
    tiles[2 * CAP : 3 * CAP] = own[...]

    def place(d, part):
        tiles[d * CAP : (d + 1) * CAP] = part[...]

    @pl.when(odd_pair == 0)
    def _():
        place(0, even)
        place(4, odd)

    @pl.when(odd_pair == 1)
    def _():
        place(0, odd)
        place(4, even)

    @pl.when(odd_core == 0)
    def _():
        place(1, core)
        place(3, side)

    @pl.when(odd_core == 1)
    def _():
        place(1, side)
        place(3, core)

    band = lax.axis_index("lat")
    updates = []
    for s in range(weight.shape[0]):
        part = lax.dot_general(
            tiles[s], weight[s], (((1,), (1,)), ((), ())), preferred_element_type=jnp.float32
        )
        source = band + REACH - s // CAP
        part = jnp.where((source >= 0) & (source < bands), part, 0.0)
        contrib[s] = part
        update = share[0] * part[0:1, :]
        for f in range(1, share.shape[0]):
            update = update + share[f] * part[f : f + 1, :]
        updates.append(update)
    for t, update in zip(goals, updates):
        y = jnp.minimum(lax.div(t, across), rows - 1)
        at = pl.ds(pl.multiple_of(lax.rem(t, across) * width, width), width)
        update = jnp.where(t < rows * across, update, 0.0)
        forced[y, :, at] = forced[y, :, at] + update

    @pl.when(odd_core == 0)
    def _():
        here[0:STEPS] = forced[rows - STEPS : rows]
        here[STEPS] = top[...]
        there[0:STEPS] = forced[0:STEPS]
        there[STEPS] = bottom[...]

    @pl.when(odd_core == 1)
    def _():
        here[0:STEPS] = forced[0:STEPS]
        here[STEPS] = bottom[...]
        there[0:STEPS] = forced[rows - STEPS : rows]
        there[STEPS] = top[...]


def land_flux(recv, contrib, flux, landed):
    fields, rows, cols = flux.shape
    width = contrib.shape[2]
    across = cols // width
    landed[...] = jnp.zeros_like(landed)
    for s in range(contrib.shape[0]):
        t = recv[0, 0, s]
        y = jnp.minimum(lax.div(t, across), rows - 1)
        k = lax.rem(t, across)
        part = jnp.where(t < rows * across, contrib[s], 0.0)
        landed[k, y] = landed[k, y] + part
    for k in range(across):
        for y in range(0, rows, SUB):
            block = jnp.swapaxes(landed[k, y : y + SUB], 0, 1)
            flux[:, y : y + SUB, k * width : (k + 1) * width] = block


def slot_masks(slots):
    wide = LANES // slots
    lane = lax.broadcasted_iota(jnp.int32, (1, LANES), 1)
    slot = lax.rem(lax.div(lane + wide // 2, wide), slots)
    place = lax.rem(lane + wide // 2, wide)
    return lane, slot, place, wide


def rolled(x, by):
    by = by % LANES
    return pltpu.roll(x, by, 1) if by else x


def slotted(row, i, wide, place):
    first = rolled(row[:, 0:LANES], wide * i + STEPS)
    last = rolled(row[:, row.shape[1] - LANES :], wide * i - STEPS)
    return jnp.where(place < wide // 2, last, first)


FIRST, LAST = STEPS, -2 * STEPS


def inside_kernel(forced, across, coef, pre, packed, even, odd, buffers):
    rows, levels, cols = forced.shape
    slots = rows // SUB
    lane, slot, place, wide = slot_masks(slots)
    for part, base in ((forced, 0), (across, levels)):
        for l in range(0, part.shape[1], SUB):
            for q in range(SUB):
                tile = None
                for i in range(slots):
                    piece = slotted(part[SUB * i + q, l : l + SUB, :], i, wide, place)
                    tile = piece if tile is None else jnp.where(slot == i, piece, tile)
                packed[q, base + l : base + l + SUB, :] = tile

    turn = lax.div(lax.rem(jnp.broadcast_to(lane, (SUB, LANES)), wide), STEPS)
    odd_block = lax.rem(lax.axis_index("lon"), 2)

    def columns(begin, target):
        for l in range(0, packed.shape[1], SUB):
            at = slice(l, l + SUB)
            total = rolled(packed[0, at], -begin)
            for q in range(1, SUB):
                total = jnp.where(turn == q, rolled(packed[q, at], STEPS * q - begin), total)
            target[at, :] = total

    @pl.when(odd_block == 0)
    def _():
        columns(LAST, even)
        columns(FIRST, odd)

    @pl.when(odd_block == 1)
    def _():
        columns(FIRST, even)
        columns(LAST, odd)

    size = rows - 2 * (SUB - STEPS)
    run_band(size, lambda n: forced[SUB - STEPS + n], coef, SUB - STEPS, buffers, pre, SUB)


def lane_reversed(x):
    tiles = []
    for k in range(x.shape[-1] // LANES - 1, -1, -1):
        block = x[:, k * LANES : (k + 1) * LANES]
        index = LANES - 1 - lax.broadcasted_iota(jnp.int32, block.shape, 1)
        tiles.append(jnp.take_along_axis(block, index, axis=1))
    return tiles


SIGNS = (1.0, -1.0, -1.0, 1.0)


def pack_kernel(
    top_band, slots, here, there, even_in, odd_in, halo, static_halo, outer, even, odd
):
    levels, cols = halo.shape[1:]
    odd_core, _ = band_parity()
    band = lax.axis_index("lat")
    fold = band == top_band - 1

    def straight(base, part):
        halo[base : base + STEPS] = part[0:STEPS]
        for f in range(4):
            static_halo[f, base : base + STEPS, :] = part[STEPS, f * STEPS : (f + 1) * STEPS, :]

    def folded(part):
        for i in range(STEPS):
            for l in range(0, levels, SUB):
                for n, block in enumerate(lane_reversed(part[STEPS - 1 - i, l : l + SUB, :])):
                    halo[i, l : l + SUB, n * LANES : (n + 1) * LANES] = block
        for r in range(0, 4 * STEPS, SUB):
            for n, block in enumerate(lane_reversed(part[STEPS, r : r + SUB, :])):
                for k in range(SUB):
                    f, i = divmod(r + k, STEPS)
                    static_halo[
                        f, STEPS - 1 - i : STEPS - i, n * LANES : (n + 1) * LANES
                    ] = SIGNS[f] * block[k : k + 1, :]

    @pl.when(odd_core == 0)
    def _():
        straight(0, here)

        @pl.when(band > 0)
        def _():
            straight(STEPS, there)

        @pl.when(band == 0)
        def _():
            halo[STEPS : 2 * STEPS] = jnp.zeros((STEPS, levels, cols), jnp.float32)
            for f in range(4):
                static_halo[f, STEPS : 2 * STEPS, :] = jnp.zeros((STEPS, cols), jnp.float32)

    @pl.when(odd_core == 1)
    def _():
        straight(STEPS, here)

        @pl.when(fold)
        def _():
            folded(there)

        @pl.when(jnp.logical_not(fold))
        def _():
            straight(0, there)

    lane, slot, place, wide = slot_masks(slots)
    zero = jnp.zeros((SUB, cols), jnp.float32)
    stacked = jnp.stack([static_halo[f] for f in range(4)] + [zero] * (SUB - 4))
    statics = jnp.swapaxes(stacked, 0, 1)
    for m in range(STEPS):
        for l in range(0, levels + SUB, SUB):
            if l < levels:
                above, below = halo[m, l : l + SUB, :], halo[STEPS + m, l : l + SUB, :]
            else:
                above, below = statics[m], statics[STEPS + m]
            north = slotted(above, slots - 1, wide, place)
            south = slotted(below, 0, wide, place)
            outer[m, l : l + SUB, :] = jnp.where(slot == 0, south, north)

    depth = even_in.shape[0]
    spot = lax.div(jnp.broadcast_to(lane, (SUB, LANES)), STEPS)
    odd_block = lax.rem(lax.axis_index("lon"), 2)
    even[0:depth, :] = even_in[...]
    odd[0:depth, :] = odd_in[...]

    def columns(begin, target):
        total = None
        for a in range(depth // SUB):
            for m in range(STEPS):
                tile = outer[m, a * SUB : (a + 1) * SUB]
                k = a * (wide // STEPS) + m
                for slot_of, where in ((slots - 1, k), (0, k + STEPS)):
                    piece = rolled(tile, STEPS * where - begin - wide * slot_of)
                    total = piece if total is None else jnp.where(spot == where, piece, total)
        target[depth : depth + SUB, :] = total

    @pl.when(odd_block == 0)
    def _():
        columns(LAST, even)
        columns(FIRST, odd)

    @pl.when(odd_block == 1)
    def _():
        columns(FIRST, even)
        columns(LAST, odd)


def bands_kernel(
    recv, contrib, forced, halo, fields, static_halo, held, pre, flux_hbm,
    coef, buffers, landed, flux, sem,
):
    rows, levels, cols = forced.shape
    del held
    land_flux(recv, contrib, flux, landed)
    copy = pltpu.make_async_copy(flux, flux_hbm, sem)
    copy.start()

    @region
    def _():
        size = SUB + 2 * STEPS
        low = [
            jnp.concatenate([static_halo[f, STEPS : 2 * STEPS], fields[f, 0 : size - STEPS]], axis=0)
            for f in range(4)
        ]
        high = [
            jnp.concatenate([fields[f, rows - size + STEPS : rows], static_halo[f, 0:STEPS]], axis=0)
            for f in range(4)
        ]
        for b, parts in enumerate((low, high)):
            for m, value in enumerate(band_stencil(parts)):
                coef[m, b * size : (b + 1) * size, :] = value

        def low_row(n):
            return halo[STEPS + n] if n < STEPS else forced[n - STEPS]

        def high_row(n):
            y = rows - size + STEPS + n
            return forced[y] if y < rows else halo[y - rows]

        run_band(size, low_row, coef, 0, buffers.at[0], pre, 0)
        run_band(size, high_row, coef, size, buffers.at[1], pre, rows - SUB)

    copy.wait()


def edge_kernel(pre, packed, outer, even, odd, out, tiles, fixed, coef, stage, sems):
    levels, rows, cols = pre.shape
    slots = rows // SUB
    lane, slot, place, wide = slot_masks(slots)
    odd_block = lax.rem(lax.axis_index("lon"), 2)
    depth = levels + SUB
    count = SUB + 2 * STEPS
    lane = jnp.broadcast_to(lane, (SUB, LANES))
    east_even = jnp.broadcast_to(odd_block == 0, (SUB, LANES))
    from_east = lax.div(place, STEPS) == wide // 2 // STEPS - 1
    from_west = lax.div(place, STEPS) == wide // 2 // STEPS

    def ends(at):
        return (
            jnp.where(east_even, even[at], odd[at]),
            jnp.where(east_even, odd[at], even[at]),
        )

    def joined(pair, tile, shift):
        tile = jnp.where(from_east, rolled(pair[0], shift - STEPS), tile)
        return jnp.where(from_west, rolled(pair[1], shift), tile)

    far = ends(slice(depth, depth + SUB))
    for a in range(depth // SUB):
        at = slice(a * SUB, (a + 1) * SUB)
        pair = ends(at)
        inner = [joined(pair, packed[q, at], -STEPS * q) for q in range(SUB)]
        placed = [None] * count
        for m in range(STEPS):
            k = STEPS * (a * (wide // STEPS) + m)
            north = joined(far, outer[m, at], wide * (slots - 1) - k)
            south = joined(far, outer[m, at], -k - STEPS * STEPS)
            placed[STEPS + SUB + m] = jnp.where(slot == slots - 1, north, rolled(inner[m], -wide))
            placed[m] = jnp.where(slot == 0, south, rolled(inner[SUB - STEPS + m], wide))
        placed[STEPS : STEPS + SUB] = inner
        for n in range(count):
            if a * SUB < levels:
                tiles[0, n, at] = placed[n]
            else:
                fixed[n * SUB : (n + 1) * SUB, :] = placed[n]

    fields = [fixed[pl.ds(f, count, stride=SUB), :] for f in range(4)]
    for m, value in enumerate(band_stencil(fields)):
        coef[m] = value
    for step in range(1, STEPS + 1):
        src, dst = (step - 1) % 2, step % 2
        for n in range(step, count - step):
            k = [jnp.broadcast_to(coef[m, n : n + 1, :], (SUB, LANES)) for m in range(5)]
            for l in range(0, levels, SUB):
                at = slice(l, l + SUB)
                c = tiles[src, n, at]
                tiles[dst, n, at] = (
                    k[0] * c
                    + k[1] * rolled(c, -1)
                    + k[2] * rolled(c, 1)
                    + k[3] * tiles[src, n + 1, at]
                    + k[4] * tiles[src, n - 1, at]
                )
    final = STEPS % 2
    copies = []
    group = 4
    for l in range(0, levels, group):
        part = slice(l, l + group)
        copy = pltpu.make_async_copy(stage.at[part], out.at[part], sems.at[l // group])
        copies.append(copy)

        @region
        def _(l=l, copy=copy):
            at = slice(l // SUB * SUB, l // SUB * SUB + SUB)
            block = jnp.stack([tiles[final, STEPS + q, at] for q in range(SUB)])
            turned = jnp.swapaxes(block, 0, 1)
            for k in range(l, l + group):
                tile = turned[k % SUB]
                for i in range(slots):
                    y = slice(i * SUB, (i + 1) * SUB)
                    low = rolled(tile, -(wide * i + STEPS))
                    high = rolled(tile, -(wide * i - STEPS))
                    body = pre[k, y, :]
                    stage[k, y, 0:LANES] = jnp.where(lane < STEPS, low, body[:, 0:LANES])
                    for x in range(LANES, cols - LANES, LANES):
                        stage[k, y, x : x + LANES] = body[:, x : x + LANES]
                    stage[k, y, cols - LANES : cols] = jnp.where(
                        lane >= LANES - STEPS, high, body[:, cols - LANES : cols]
                    )
            copy.start()

    for copy in copies:
        copy.wait()


def body(
    atm_flux,
    send_tile,
    recv_tile,
    remap_weight,
    tracer,
    diffusivity,
    zonal_velocity,
    merid_velocity,
    ocean_mask,
    level_proj,
):
    bands, blocks = lax.axis_size("lat"), lax.axis_size("lon")
    fields, width = atm_flux.shape[2:]
    levels, rows, cols = tracer.shape
    slots = remap_weight.shape[0]
    f32, bf16 = jnp.float32, jnp.bfloat16
    statics = (diffusivity, zonal_velocity, merid_velocity, ocean_mask)

    core_pairs = swaps([(i, i + 1) for i in range(0, bands, 2)])
    chips = [(i, i + 1) for i in range(bands // 2 - 1)]
    even_chips = filled(swaps([(2 * a + k, 2 * b + k) for a, b in chips[0::2] for k in (0, 1)]), bands)
    odd_chips = filled(swaps([(2 * a + k, 2 * b + k) for a, b in chips[1::2] for k in (0, 1)]), bands)
    last = (bands - 1) * blocks
    beside = swaps(
        [(i * blocks + j, (i + 1) * blocks + j) for i in range(1, bands - 1, 2) for j in range(blocks)]
    )
    fold = [(last + j, last + blocks - 1 - j) for j in range(blocks)]
    def ends(band, kind):
        at = [band * blocks + j for j in range(blocks)]
        h = blocks // 2
        if kind == "x":
            return swaps(list(zip(at[0::2], at[1::2])))
        if kind == "y":
            return swaps(list(zip(at[:h], at[h:])))
        return swaps(list(zip(at[:h], at[::-1][:h])))

    across_chips = beside + fold + ends(0, "y")
    beside = beside + ends(0, "x") + ends(bands - 1, "x")
    even_blocks = swaps([(j, j + 1) for j in range(0, blocks, 2)])
    odd_blocks = swaps([(j, (j + 1) % blocks) for j in range(1, blocks, 2)])

    tile2 = ((CAP, fields, width), bf16)
    core, side, even, odd, own = call(
        gather_kernel,
        [tile2] * 5,
        [HB, HB],
        "gather",
        scratch=[
            pltpu.SMEM(send_tile.shape, jnp.int32),
            pltpu.VMEM(atm_flux.shape, bf16),
            pltpu.SemaphoreType.DMA((2,)),
        ],
    )(*in_hbm(send_tile, atm_flux))
    core = traded(core, "lat", core_pairs, "tile_core")
    even = traded(even, "lat", even_chips, "tile_even")
    odd = traded(odd, "lat", odd_chips, "tile_odd")
    side = traded(side, ("lat", "lon"), beside, "tile_side")
    start, across, top, bottom, parts, coef, weight, share, recv = call(
        prepare_kernel,
        [
            ((rows, levels, cols), f32),
            ((rows, SUB, cols), f32),
            ((4 * STEPS, cols), f32),
            ((4 * STEPS, cols), f32),
            ((4, rows, cols), f32),
            ((5, rows, cols), f32),
            (remap_weight.shape, bf16),
            ((fields, levels, width), f32),
            (recv_tile.shape, jnp.int32),
        ],
        [HB] * 8,
        "prepare",
        scratch=[
            pltpu.VMEM(tracer.shape, f32),
            pltpu.VMEM((rows, cols), jnp.int32),
            pltpu.VMEM((fields, levels), f32),
            pltpu.SemaphoreType.DMA((8,)),
        ],
    )(*in_hbm(tracer, *statics, remap_weight, level_proj.T, recv_tile))
    ring = ((STEPS + 1, levels, cols), f32)
    forced, contrib, here, there = call(
        functools.partial(remap_kernel, bands),
        [((rows, levels, cols), f32), ((slots, fields, width), f32), ring, ring],
        [VM] * 11,
        "remap",
        scratch=[
            pltpu.VMEM((slots, fields, width), bf16),
        ],
        aliases={8: 0},
    )(recv, own, core, side, even, odd, weight, share, start, top, bottom)
    here = traded(here, "lat", core_pairs, "lat_core")
    there = traded(there, ("lat", "lon"), across_chips, "lat_chip")
    depth = levels + SUB
    count = SUB + 2 * STEPS
    pre, packed, even, odd = call(
        inside_kernel,
        [
            ((levels, rows, cols), f32),
            ((SUB, depth, LANES), f32),
            ((depth, LANES), f32),
            ((depth, LANES), f32),
        ],
        [VM] * 3,
        "inside",
        scratch=[pltpu.VMEM((2, rows, levels, cols), f32)],
    )(forced, across, coef)
    halo, static_halo, outer, even, odd = call(
        functools.partial(pack_kernel, bands, rows // SUB),
        [
            ((2 * STEPS, levels, cols), f32),
            ((4, 2 * STEPS, cols), f32),
            ((STEPS, depth, LANES), f32),
            ((depth + SUB, LANES), f32),
            ((depth + SUB, LANES), f32),
        ],
        [VM] * 4,
        "pack",
    )(here, there, even, odd)
    even = traded(even, "lon", even_blocks, "lon_even")
    odd = traded(odd, "lon", odd_blocks, "lon_odd")
    pre, ocean_flux = call(
        bands_kernel,
        [((levels, rows, cols), f32), ((fields, rows, cols), f32)],
        [SM] + [VM] * 6,
        "bands",
        scratch=[
            pltpu.VMEM((5, 2 * count, cols), f32),
            pltpu.VMEM((2, 2, count, levels, cols), f32),
            pltpu.VMEM((cols // width, rows, fields, width), f32),
            pltpu.VMEM((fields, rows, cols), f32),
            pltpu.SemaphoreType.DMA(()),
        ],
        aliases={6: 0},
        out_specs=[VM, HB],
    )(recv, contrib, forced, halo, parts, static_halo, pre)
    (out,) = call(
        edge_kernel,
        [((levels, rows, cols), f32)],
        [VM] * 5,
        "edges",
        scratch=[
            pltpu.VMEM((2, count, levels, LANES), f32),
            pltpu.VMEM((count * SUB, LANES), f32),
            pltpu.VMEM((5, count, LANES), f32),
            pltpu.VMEM((levels, rows, cols), f32),
            pltpu.SemaphoreType.DMA((levels // 4,)),
        ],
        out_specs=[HB],
    )(pre, packed, outer, even, odd)
    return (ocean_flux, out)


def solution(mesh):
    placed = (
        P("lat", None, None, "lon"),
        P("lat", "lon", None),
        P("lat", "lon", None),
        P("lat", None, "lon"),
        P(None, "lat", "lon"),
        P("lat", "lon"),
        P("lat", "lon"),
        P("lat", "lon"),
        P("lat", "lon"),
        P(),
    )
    return jax.shard_map(
        body,
        mesh=mesh,
        in_specs=placed,
        out_specs=(P(None, "lat", "lon"), P(None, "lat", "lon")),
        check_vma=False,
    )
```

```python
import functools

import jax
import jax.numpy as jnp
from jax import lax
from jax.experimental import pallas as pl
from jax.experimental.pallas import tpu as pltpu
from jax.sharding import PartitionSpec as P

CAP = 2
REACH = 2
STEPS = 4
LANES = 128
SUB = 8

VM = pl.BlockSpec(memory_space=pltpu.VMEM)
SM = pl.BlockSpec(memory_space=pltpu.SMEM)
HB = pl.BlockSpec(memory_space=pltpu.HBM)


def call(kernel, outs, in_specs, name, scratch=(), aliases=None, limit=12, out_specs=None):
    run = pl.pallas_call(
        kernel,
        out_shape=[jax.ShapeDtypeStruct(s, d) for s, d in outs],
        in_specs=in_specs,
        out_specs=out_specs or [VM] * len(outs),
        scratch_shapes=list(scratch),
        input_output_aliases=aliases or {},
        compiler_params=pltpu.CompilerParams(vmem_limit_bytes=limit << 20),
        name=name,
    )

    def scoped(*args):
        with jax.named_scope("run_" + name):
            return run(*args)

    return scoped


def in_hbm(*arrays):
    return [pltpu.with_memory_space_constraint(x, pltpu.HBM) for x in arrays]


def filled(routes, size):
    busy = {a for a, _ in routes}
    free = [i for i in range(size) if i not in busy]
    return routes + swaps(list(zip(free[0::2], free[1::2])))


def traded(x, axis, pairs, name):
    with jax.named_scope(name):
        return lax.ppermute(x, axis, pairs)


def swaps(pairs):
    return [route for a, b in pairs for route in ((a, b), (b, a))]


def region(step):
    pl.when(lax.axis_index("lat") >= 0)(step)


def band_parity():
    band = lax.axis_index("lat")
    return lax.rem(band, 2), lax.rem(lax.div(band, 2), 2)


def gather_kernel(send_hbm, atm_hbm, core, side, even, odd, own, send, atm, sems):
    copies = [
        pltpu.make_async_copy(send_hbm, send, sems.at[0]),
        pltpu.make_async_copy(atm_hbm, atm, sems.at[1]),
    ]
    for copy in copies:
        copy.start()
    for copy in copies:
        copy.wait()
    odd_core, odd_pair = band_parity()
    goes = (
        (core, 3 - 2 * odd_core),
        (side, 1 + 2 * odd_core),
        (even, 4 - 4 * odd_pair),
        (odd, 4 * odd_pair),
        (own, 2),
    )
    for target, d in goes:
        for c in range(CAP):
            target[c] = atm[0, send[0, 0, d * CAP + c]]


def faces(vel, d, wet, vel_next, d_next, wet_next):
    w = wet * wet_next
    speed = 0.5 * (vel + vel_next) * w
    mix = 0.5 * (d + d_next) * w
    return jnp.maximum(speed, 0.0) + mix, jnp.minimum(speed, 0.0) - mix


def stencil(wet, east, west, north, south):
    center = 1.0 - wet * (east[0] - west[1] + north[0] - south[1])
    return center, -wet * east[1], wet * west[0], -wet * north[1], wet * south[0]


def band_stencil(fields):
    d, u, v, wet = fields
    cols = d.shape[1]

    def moved(x, by, axis):
        if axis:
            return pltpu.roll(x, by % cols, 1)
        return jnp.concatenate([x[-by:], x[:-by]], axis=0)

    east = faces(u, d, wet, *(moved(x, -1, 1) for x in (u, d, wet)))
    north = faces(v, d, wet, *(moved(x, -1, 0) for x in (v, d, wet)))
    west = tuple(moved(x, 1, 1) for x in east)
    south = tuple(moved(x, 1, 0) for x in north)
    return stencil(wet, east, west, north, south)


def run_band(size, read, coef, base, buffers, pre, target):
    levels, _, cols = pre.shape
    src = read
    for step in range(1, STEPS + 1):
        new = []
        for n in range(step, size - step):
            c = src(n)
            k = [
                jnp.broadcast_to(coef[m, base + n : base + n + 1, :], (levels, cols))
                for m in range(5)
            ]
            value = (
                k[0] * c
                + k[1] * pltpu.roll(c, cols - 1, 1)
                + k[2] * pltpu.roll(c, 1, 1)
                + k[3] * src(n + 1)
                + k[4] * src(n - 1)
            )
            if step < STEPS:
                buffers[step % 2, n] = value
            else:
                new.append(value)
                if len(new) == SUB:
                    block = jnp.stack(new)
                    at = target + n - STEPS - SUB + 1
                    for l in range(0, levels, SUB):
                        pre[l : l + SUB, at : at + SUB, :] = jnp.swapaxes(
                            block[:, l : l + SUB], 0, 1
                        )
                    new = []
        src = lambda n, held=buffers.at[step % 2]: held[n]


def prepare_kernel(
    tracer_hbm, diff_hbm, zonal_hbm, merid_hbm, mask_hbm, weight_hbm, proj_hbm, recv_hbm,
    rows_out, across, top, bottom, fields, coef, weight, share, recv,
    tracer, mask, proj, sems,
):
    levels, rows, cols = tracer.shape
    sources = (tracer_hbm, diff_hbm, zonal_hbm, merid_hbm, mask_hbm, proj_hbm, weight_hbm, recv_hbm)
    targets = (tracer, fields.at[0], fields.at[1], fields.at[2], mask, proj, weight, recv)
    copies = [pltpu.make_async_copy(a, b, sems.at[k]) for k, (a, b) in enumerate(zip(sources, targets))]
    for copy in copies:
        copy.start()
    for copy in copies[1:6]:
        copy.wait()
    fields[3] = mask[...].astype(jnp.float32)
    for f in range(share.shape[0]):
        share[f] = jnp.broadcast_to(jnp.swapaxes(proj[f : f + 1, :], 0, 1), share.shape[1:])
    parts = [fields[f] for f in range(4)]
    zero = jnp.zeros((SUB, cols), jnp.float32)
    for y in range(0, rows, SUB):
        stacked = jnp.stack([x[y : y + SUB] for x in parts] + [zero] * (SUB - 4))
        across[y : y + SUB] = jnp.swapaxes(stacked, 0, 1)
    for f, x in enumerate(parts):
        bottom[f * STEPS : (f + 1) * STEPS, :] = x[0:STEPS]
        top[f * STEPS : (f + 1) * STEPS, :] = x[rows - STEPS : rows]
    for m, value in enumerate(band_stencil(parts)):
        coef[m] = value
    copies[0].wait()
    for y in range(0, rows, SUB):
        for l in range(0, levels, SUB):
            block = tracer[l : l + SUB, y : y + SUB, :]
            rows_out[y : y + SUB, l : l + SUB, :] = jnp.swapaxes(block, 0, 1)
    copies[6].wait()
    copies[7].wait()


def remap_kernel(
    bands, recv, own, core, side, even, odd, weight, share, start, top, bottom,
    forced, contrib, here, there, tiles,
):
    goal = recv[0].astype(jnp.float32)
    index = lax.broadcasted_iota(jnp.int32, goal.shape, 1)
    goals = [jnp.sum(jnp.where(index == s, goal, 0.0)).astype(jnp.int32) for s in range(goal.shape[1])]
    rows, levels, cols = forced.shape
    width = weight.shape[1]
    across = cols // width
    odd_core, odd_pair = band_parity()
    tiles[2 * CAP : 3 * CAP] = own[...]

    def place(d, part):
        tiles[d * CAP : (d + 1) * CAP] = part[...]

    @pl.when(odd_pair == 0)
    def _():
        place(0, even)
        place(4, odd)

    @pl.when(odd_pair == 1)
    def _():
        place(0, odd)
        place(4, even)

    @pl.when(odd_core == 0)
    def _():
        place(1, core)
        place(3, side)

    @pl.when(odd_core == 1)
    def _():
        place(1, side)
        place(3, core)

    band = lax.axis_index("lat")
    updates = []
    for s in range(weight.shape[0]):
        part = lax.dot_general(
            tiles[s], weight[s], (((1,), (1,)), ((), ())), preferred_element_type=jnp.float32
        )
        source = band + REACH - s // CAP
        part = jnp.where((source >= 0) & (source < bands), part, 0.0)
        contrib[s] = part
        update = share[0] * part[0:1, :]
        for f in range(1, share.shape[0]):
            update = update + share[f] * part[f : f + 1, :]
        updates.append(update)
    for t, update in zip(goals, updates):
        y = jnp.minimum(lax.div(t, across), rows - 1)
        at = pl.ds(pl.multiple_of(lax.rem(t, across) * width, width), width)
        update = jnp.where(t < rows * across, update, 0.0)
        forced[y, :, at] = forced[y, :, at] + update

    @pl.when(odd_core == 0)
    def _():
        here[0:STEPS] = forced[rows - STEPS : rows]
        here[STEPS] = top[...]
        there[0:STEPS] = forced[0:STEPS]
        there[STEPS] = bottom[...]

    @pl.when(odd_core == 1)
    def _():
        here[0:STEPS] = forced[0:STEPS]
        here[STEPS] = bottom[...]
        there[0:STEPS] = forced[rows - STEPS : rows]
        there[STEPS] = top[...]


def land_flux(recv, contrib, flux, landed):
    fields, rows, cols = flux.shape
    width = contrib.shape[2]
    across = cols // width
    landed[...] = jnp.zeros_like(landed)
    for s in range(contrib.shape[0]):
        t = recv[0, 0, s]
        y = jnp.minimum(lax.div(t, across), rows - 1)
        k = lax.rem(t, across)
        part = jnp.where(t < rows * across, contrib[s], 0.0)
        landed[k, y] = landed[k, y] + part
    for k in range(across):
        for y in range(0, rows, SUB):
            block = jnp.swapaxes(landed[k, y : y + SUB], 0, 1)
            flux[:, y : y + SUB, k * width : (k + 1) * width] = block


def slot_masks(slots):
    wide = LANES // slots
    lane = lax.broadcasted_iota(jnp.int32, (1, LANES), 1)
    slot = lax.rem(lax.div(lane + wide // 2, wide), slots)
    place = lax.rem(lane + wide // 2, wide)
    return lane, slot, place, wide


def rolled(x, by):
    by = by % LANES
    return pltpu.roll(x, by, 1) if by else x


def slotted(row, i, wide, place):
    first = rolled(row[:, 0:LANES], wide * i + STEPS)
    last = rolled(row[:, row.shape[1] - LANES :], wide * i - STEPS)
    return jnp.where(place < wide // 2, last, first)


FIRST, LAST = STEPS, -2 * STEPS


def inside_kernel(forced, across, coef, pre, packed, even, odd, buffers):
    rows, levels, cols = forced.shape
    slots = rows // SUB
    lane, slot, place, wide = slot_masks(slots)
    for part, base in ((forced, 0), (across, levels)):
        for l in range(0, part.shape[1], SUB):
            for q in range(SUB):
                tile = None
                for i in range(slots):
                    piece = slotted(part[SUB * i + q, l : l + SUB, :], i, wide, place)
                    tile = piece if tile is None else jnp.where(slot == i, piece, tile)
                packed[q, base + l : base + l + SUB, :] = tile

    turn = lax.div(lax.rem(jnp.broadcast_to(lane, (SUB, LANES)), wide), STEPS)
    odd_block = lax.rem(lax.axis_index("lon"), 2)

    def columns(begin, target):
        for l in range(0, packed.shape[1], SUB):
            at = slice(l, l + SUB)
            total = rolled(packed[0, at], -begin)
            for q in range(1, SUB):
                total = jnp.where(turn == q, rolled(packed[q, at], STEPS * q - begin), total)
            target[at, :] = total

    @pl.when(odd_block == 0)
    def _():
        columns(LAST, even)
        columns(FIRST, odd)

    @pl.when(odd_block == 1)
    def _():
        columns(FIRST, even)
        columns(LAST, odd)

    size = rows - 2 * (SUB - STEPS)
    run_band(size, lambda n: forced[SUB - STEPS + n], coef, SUB - STEPS, buffers, pre, SUB)


def lane_reversed(x):
    tiles = []
    for k in range(x.shape[-1] // LANES - 1, -1, -1):
        block = x[:, k * LANES : (k + 1) * LANES]
        index = LANES - 1 - lax.broadcasted_iota(jnp.int32, block.shape, 1)
        tiles.append(jnp.take_along_axis(block, index, axis=1))
    return tiles


SIGNS = (1.0, -1.0, -1.0, 1.0)


def pack_kernel(
    top_band, slots, here, there, even_in, odd_in, halo, static_halo, outer, even, odd
):
    levels, cols = halo.shape[1:]
    odd_core, _ = band_parity()
    band = lax.axis_index("lat")
    fold = band == top_band - 1

    def straight(base, part):
        halo[base : base + STEPS] = part[0:STEPS]
        for f in range(4):
            static_halo[f, base : base + STEPS, :] = part[STEPS, f * STEPS : (f + 1) * STEPS, :]

    def folded(part):
        for i in range(STEPS):
            for l in range(0, levels, SUB):
                for n, block in enumerate(lane_reversed(part[STEPS - 1 - i, l : l + SUB, :])):
                    halo[i, l : l + SUB, n * LANES : (n + 1) * LANES] = block
        for r in range(0, 4 * STEPS, SUB):
            for n, block in enumerate(lane_reversed(part[STEPS, r : r + SUB, :])):
                for k in range(SUB):
                    f, i = divmod(r + k, STEPS)
                    static_halo[
                        f, STEPS - 1 - i : STEPS - i, n * LANES : (n + 1) * LANES
                    ] = SIGNS[f] * block[k : k + 1, :]

    @pl.when(odd_core == 0)
    def _():
        straight(0, here)

        @pl.when(band > 0)
        def _():
            straight(STEPS, there)

        @pl.when(band == 0)
        def _():
            halo[STEPS : 2 * STEPS] = jnp.zeros((STEPS, levels, cols), jnp.float32)
            for f in range(4):
                static_halo[f, STEPS : 2 * STEPS, :] = jnp.zeros((STEPS, cols), jnp.float32)

    @pl.when(odd_core == 1)
    def _():
        straight(STEPS, here)

        @pl.when(fold)
        def _():
            folded(there)

        @pl.when(jnp.logical_not(fold))
        def _():
            straight(0, there)

    lane, slot, place, wide = slot_masks(slots)
    zero = jnp.zeros((SUB, cols), jnp.float32)
    stacked = jnp.stack([static_halo[f] for f in range(4)] + [zero] * (SUB - 4))
    statics = jnp.swapaxes(stacked, 0, 1)
    for m in range(STEPS):
        for l in range(0, levels + SUB, SUB):
            if l < levels:
                above, below = halo[m, l : l + SUB, :], halo[STEPS + m, l : l + SUB, :]
            else:
                above, below = statics[m], statics[STEPS + m]
            north = slotted(above, slots - 1, wide, place)
            south = slotted(below, 0, wide, place)
            outer[m, l : l + SUB, :] = jnp.where(slot == 0, south, north)

    depth = even_in.shape[0]
    spot = lax.div(jnp.broadcast_to(lane, (SUB, LANES)), STEPS)
    odd_block = lax.rem(lax.axis_index("lon"), 2)
    even[0:depth, :] = even_in[...]
    odd[0:depth, :] = odd_in[...]

    def columns(begin, target):
        total = None
        for a in range(depth // SUB):
            for m in range(STEPS):
                tile = outer[m, a * SUB : (a + 1) * SUB]
                k = a * (wide // STEPS) + m
                for slot_of, where in ((slots - 1, k), (0, k + STEPS)):
                    piece = rolled(tile, STEPS * where - begin - wide * slot_of)
                    total = piece if total is None else jnp.where(spot == where, piece, total)
        target[depth : depth + SUB, :] = total

    @pl.when(odd_block == 0)
    def _():
        columns(LAST, even)
        columns(FIRST, odd)

    @pl.when(odd_block == 1)
    def _():
        columns(FIRST, even)
        columns(LAST, odd)


def bands_kernel(
    recv, contrib, forced, halo, fields, static_halo, held, pre, flux_hbm,
    coef, buffers, landed, flux, sem,
):
    rows, levels, cols = forced.shape
    del held
    land_flux(recv, contrib, flux, landed)
    copy = pltpu.make_async_copy(flux, flux_hbm, sem)
    copy.start()

    @region
    def _():
        size = SUB + 2 * STEPS
        low = [
            jnp.concatenate([static_halo[f, STEPS : 2 * STEPS], fields[f, 0 : size - STEPS]], axis=0)
            for f in range(4)
        ]
        high = [
            jnp.concatenate([fields[f, rows - size + STEPS : rows], static_halo[f, 0:STEPS]], axis=0)
            for f in range(4)
        ]
        for b, parts in enumerate((low, high)):
            for m, value in enumerate(band_stencil(parts)):
                coef[m, b * size : (b + 1) * size, :] = value

        def low_row(n):
            return halo[STEPS + n] if n < STEPS else forced[n - STEPS]

        def high_row(n):
            y = rows - size + STEPS + n
            return forced[y] if y < rows else halo[y - rows]

        run_band(size, low_row, coef, 0, buffers.at[0], pre, 0)
        run_band(size, high_row, coef, size, buffers.at[1], pre, rows - SUB)

    copy.wait()


def edge_kernel(pre, packed, outer, even, odd, out, tiles, fixed, coef, stage, sems):
    levels, rows, cols = pre.shape
    slots = rows // SUB
    lane, slot, place, wide = slot_masks(slots)
    odd_block = lax.rem(lax.axis_index("lon"), 2)
    depth = levels + SUB
    count = SUB + 2 * STEPS
    lane = jnp.broadcast_to(lane, (SUB, LANES))
    east_even = jnp.broadcast_to(odd_block == 0, (SUB, LANES))
    from_east = lax.div(place, STEPS) == wide // 2 // STEPS - 1
    from_west = lax.div(place, STEPS) == wide // 2 // STEPS

    def ends(at):
        return (
            jnp.where(east_even, even[at], odd[at]),
            jnp.where(east_even, odd[at], even[at]),
        )

    def joined(pair, tile, shift):
        tile = jnp.where(from_east, rolled(pair[0], shift - STEPS), tile)
        return jnp.where(from_west, rolled(pair[1], shift), tile)

    far = ends(slice(depth, depth + SUB))
    for a in range(depth // SUB - 1, -1, -1):

        @region
        def _(a=a):
            at = slice(a * SUB, (a + 1) * SUB)
            pair = ends(at)
            inner = [joined(pair, packed[q, at], -STEPS * q) for q in range(SUB)]
            placed = [None] * count
            for m in range(STEPS):
                k = STEPS * (a * (wide // STEPS) + m)
                north = joined(far, outer[m, at], wide * (slots - 1) - k)
                south = joined(far, outer[m, at], -k - STEPS * STEPS)
                placed[STEPS + SUB + m] = jnp.where(slot == slots - 1, north, rolled(inner[m], -wide))
                placed[m] = jnp.where(slot == 0, south, rolled(inner[SUB - STEPS + m], wide))
            placed[STEPS : STEPS + SUB] = inner
            for n in range(count):
                if a * SUB < levels:
                    tiles[0, n, at] = placed[n]
                else:
                    fixed[n * SUB : (n + 1) * SUB, :] = placed[n]

    fields = [fixed[pl.ds(f, count, stride=SUB), :] for f in range(4)]
    for m, value in enumerate(band_stencil(fields)):
        coef[m] = value
    for step in range(1, STEPS + 1):
        src, dst = (step - 1) % 2, step % 2
        for n in range(step, count - step):
            k = [jnp.broadcast_to(coef[m, n : n + 1, :], (SUB, LANES)) for m in range(5)]
            for l in range(0, levels, SUB):
                at = slice(l, l + SUB)
                c = tiles[src, n, at]
                tiles[dst, n, at] = (
                    k[0] * c
                    + k[1] * rolled(c, -1)
                    + k[2] * rolled(c, 1)
                    + k[3] * tiles[src, n + 1, at]
                    + k[4] * tiles[src, n - 1, at]
                )
    final = STEPS % 2
    copies = []
    group = 4
    for l in range(0, levels, group):
        part = slice(l, l + group)
        copy = pltpu.make_async_copy(stage.at[part], out.at[part], sems.at[l // group])
        copies.append(copy)

        @region
        def _(l=l, copy=copy):
            at = slice(l // SUB * SUB, l // SUB * SUB + SUB)
            block = jnp.stack([tiles[final, STEPS + q, at] for q in range(SUB)])
            turned = jnp.swapaxes(block, 0, 1)
            for k in range(l, l + group):
                tile = turned[k % SUB]
                for i in range(slots):
                    y = slice(i * SUB, (i + 1) * SUB)
                    low = rolled(tile, -(wide * i + STEPS))
                    high = rolled(tile, -(wide * i - STEPS))
                    body = pre[k, y, :]
                    stage[k, y, 0:LANES] = jnp.where(lane < STEPS, low, body[:, 0:LANES])
                    for x in range(LANES, cols - LANES, LANES):
                        stage[k, y, x : x + LANES] = body[:, x : x + LANES]
                    stage[k, y, cols - LANES : cols] = jnp.where(
                        lane >= LANES - STEPS, high, body[:, cols - LANES : cols]
                    )
            copy.start()

    for copy in copies:
        copy.wait()


def body(
    atm_flux,
    send_tile,
    recv_tile,
    remap_weight,
    tracer,
    diffusivity,
    zonal_velocity,
    merid_velocity,
    ocean_mask,
    level_proj,
):
    bands, blocks = lax.axis_size("lat"), lax.axis_size("lon")
    fields, width = atm_flux.shape[2:]
    levels, rows, cols = tracer.shape
    slots = remap_weight.shape[0]
    f32, bf16 = jnp.float32, jnp.bfloat16
    statics = (diffusivity, zonal_velocity, merid_velocity, ocean_mask)

    core_pairs = swaps([(i, i + 1) for i in range(0, bands, 2)])
    chips = [(i, i + 1) for i in range(bands // 2 - 1)]
    even_chips = filled(swaps([(2 * a + k, 2 * b + k) for a, b in chips[0::2] for k in (0, 1)]), bands)
    odd_chips = filled(swaps([(2 * a + k, 2 * b + k) for a, b in chips[1::2] for k in (0, 1)]), bands)
    last = (bands - 1) * blocks
    beside = swaps(
        [(i * blocks + j, (i + 1) * blocks + j) for i in range(1, bands - 1, 2) for j in range(blocks)]
    )
    fold = [(last + j, last + blocks - 1 - j) for j in range(blocks)]
    def ends(band, kind):
        at = [band * blocks + j for j in range(blocks)]
        h = blocks // 2
        if kind == "x":
            return swaps(list(zip(at[0::2], at[1::2])))
        if kind == "y":
            return swaps(list(zip(at[:h], at[h:])))
        return swaps(list(zip(at[:h], at[::-1][:h])))

    across_chips = beside + fold + ends(0, "y")
    beside = beside + ends(0, "x") + ends(bands - 1, "x")
    even_blocks = swaps([(j, j + 1) for j in range(0, blocks, 2)])
    odd_blocks = swaps([(j, (j + 1) % blocks) for j in range(1, blocks, 2)])

    tile2 = ((CAP, fields, width), bf16)
    core, side, even, odd, own = call(
        gather_kernel,
        [tile2] * 5,
        [HB, HB],
        "gather",
        scratch=[
            pltpu.SMEM(send_tile.shape, jnp.int32),
            pltpu.VMEM(atm_flux.shape, bf16),
            pltpu.SemaphoreType.DMA((2,)),
        ],
    )(*in_hbm(send_tile, atm_flux))
    core = traded(core, "lat", core_pairs, "tile_core")
    even = traded(even, "lat", even_chips, "tile_even")
    odd = traded(odd, "lat", odd_chips, "tile_odd")
    side = traded(side, ("lat", "lon"), beside, "tile_side")
    start, across, top, bottom, parts, coef, weight, share, recv = call(
        prepare_kernel,
        [
            ((rows, levels, cols), f32),
            ((rows, SUB, cols), f32),
            ((4 * STEPS, cols), f32),
            ((4 * STEPS, cols), f32),
            ((4, rows, cols), f32),
            ((5, rows, cols), f32),
            (remap_weight.shape, bf16),
            ((fields, levels, width), f32),
            (recv_tile.shape, jnp.int32),
        ],
        [HB] * 8,
        "prepare",
        scratch=[
            pltpu.VMEM(tracer.shape, f32),
            pltpu.VMEM((rows, cols), jnp.int32),
            pltpu.VMEM((fields, levels), f32),
            pltpu.SemaphoreType.DMA((8,)),
        ],
    )(*in_hbm(tracer, *statics, remap_weight, level_proj.T, recv_tile))
    ring = ((STEPS + 1, levels, cols), f32)
    forced, contrib, here, there = call(
        functools.partial(remap_kernel, bands),
        [((rows, levels, cols), f32), ((slots, fields, width), f32), ring, ring],
        [VM] * 11,
        "remap",
        scratch=[
            pltpu.VMEM((slots, fields, width), bf16),
        ],
        aliases={8: 0},
    )(recv, own, core, side, even, odd, weight, share, start, top, bottom)
    here = traded(here, "lat", core_pairs, "lat_core")
    there = traded(there, ("lat", "lon"), across_chips, "lat_chip")
    depth = levels + SUB
    count = SUB + 2 * STEPS
    pre, packed, even, odd = call(
        inside_kernel,
        [
            ((levels, rows, cols), f32),
            ((SUB, depth, LANES), f32),
            ((depth, LANES), f32),
            ((depth, LANES), f32),
        ],
        [VM] * 3,
        "inside",
        scratch=[pltpu.VMEM((2, rows, levels, cols), f32)],
    )(forced, across, coef)
    halo, static_halo, outer, even, odd = call(
        functools.partial(pack_kernel, bands, rows // SUB),
        [
            ((2 * STEPS, levels, cols), f32),
            ((4, 2 * STEPS, cols), f32),
            ((STEPS, depth, LANES), f32),
            ((depth + SUB, LANES), f32),
            ((depth + SUB, LANES), f32),
        ],
        [VM] * 4,
        "pack",
    )(here, there, even, odd)
    even = traded(even, "lon", even_blocks, "lon_even")
    odd = traded(odd, "lon", odd_blocks, "lon_odd")
    pre, ocean_flux = call(
        bands_kernel,
        [((levels, rows, cols), f32), ((fields, rows, cols), f32)],
        [SM] + [VM] * 6,
        "bands",
        scratch=[
            pltpu.VMEM((5, 2 * count, cols), f32),
            pltpu.VMEM((2, 2, count, levels, cols), f32),
            pltpu.VMEM((cols // width, rows, fields, width), f32),
            pltpu.VMEM((fields, rows, cols), f32),
            pltpu.SemaphoreType.DMA(()),
        ],
        aliases={6: 0},
        out_specs=[VM, HB],
    )(recv, contrib, forced, halo, parts, static_halo, pre)
    (out,) = call(
        edge_kernel,
        [((levels, rows, cols), f32)],
        [VM] * 5,
        "edges",
        scratch=[
            pltpu.VMEM((2, count, levels, LANES), f32),
            pltpu.VMEM((count * SUB, LANES), f32),
            pltpu.VMEM((5, count, LANES), f32),
            pltpu.VMEM((levels, rows, cols), f32),
            pltpu.SemaphoreType.DMA((levels // 4,)),
        ],
        out_specs=[HB],
    )(pre, packed, outer, even, odd)
    return (ocean_flux, out)


def solution(mesh):
    placed = (
        P("lat", None, None, "lon"),
        P("lat", "lon", None),
        P("lat", "lon", None),
        P("lat", None, "lon"),
        P(None, "lat", "lon"),
        P("lat", "lon"),
        P("lat", "lon"),
        P("lat", "lon"),
        P("lat", "lon"),
        P(),
    )
    return jax.shard_map(
        body,
        mesh=mesh,
        in_specs=placed,
        out_specs=(P(None, "lat", "lon"), P(None, "lat", "lon")),
        check_vma=False,
    )
```
